512 devices in a mesh: region: 32 (over y, x_lo, core), grp: 16 (over z, x_hi).
Axes of the slice: x: 4 (x_hi: 2, x_lo: 2; x = x_hi * 2 + x_lo), y: 8, z: 8, core: 2. Of those that a mesh axis runs over, the one named last changes fastest.
Arguments:
- transmission: float32 [2, 640, 20480], P(None, 'grp', 'region'), may hold values from -3 to 3
- probe: bfloat16 [2, 8, 512, 512], P(None, None, 'grp'), may hold values from -1.5 to 1.5
- measured: float32 [32, 512, 512], P('region', 'grp'), may hold values from 0 to 2
- positions: int32 [32, 2], P('region'), may hold values from 0 to 128
- past_steps: float32 [4, 2, 640, 20480], P(None, None, 'grp', 'region'), may hold values from -40 to 40
- past_changes: float32 [3, 2, 640, 20480], P(None, None, 'grp', 'region'), may hold values from -240 to 240
- old_gradient: float32 [2, 640, 20480], P(None, 'grp', 'region'), may hold values from -40 to 40
Outputs:
- updated: float32 [2, 640, 20480], P(None, 'grp', 'region')
- gradient: float32 [2, 640, 20480], P(None, 'grp', 'region')
The draws below stay inside these ranges and needn't reach their ends.
All inputs are finite; a program needn't handle non-finite values.
Results may differ from the reference program's by a relative error of at most 0.019.
The reference program's roundings to bfloat16 on the way count: a program that leaves them out, or rounds other values in their place, can miss the bound.
Values may be sent and summed in bfloat16 or wider, within the bound.
A program may use at most 64 MiB of HBM per device.

```python
import math
import jax
import jax.numpy as jnp
from jax import lax

N = 512
MODES = 8
FR = 1
SPAN = 128
HIST = 4
OBJ = 640
OBJ_ALL = 20480
FRAMES = 32
N_REGION = 32


TIKHONOV = 0.5


def row_col_scale(key):
    key_rows, key_cols = jax.random.split(key)
    trend = math.log(3.0)
    place = jnp.arange(OBJ_ALL, dtype=jnp.float32) / (OBJ_ALL - 1)
    row_part = jnp.exp(trend * place + jax.random.uniform(key_rows, (OBJ_ALL,), jnp.float32, -1.15, 1.15))
    col_part = jnp.exp(jax.random.uniform(key_cols, (OBJ,), jnp.float32, -1.15, 1.15))
    return col_part[:, None] * row_part[None, :]


def history(key):
    keys = [jax.random.fold_in(key, 101 + index) for index in range(10)]
    base = jnp.clip(0.7 * jax.random.normal(keys[0], (2, OBJ, OBJ_ALL), jnp.float32), -3.0, 3.0)
    scale = row_col_scale(keys[1])
    pull = jax.random.uniform(keys[2], (HIST, 1, 1, 1), jnp.float32, 0.1, 0.5)
    noise = jax.random.normal(keys[3], (HIST, 2, OBJ, OBJ_ALL), jnp.float32)
    steps_all = jnp.clip(scale * (0.5 * noise - pull * base), -40.0, 40.0)
    curve = jnp.exp(jax.random.uniform(keys[5], (2, OBJ, OBJ_ALL), jnp.float32, math.log(0.5), math.log(2.0)))
    weak_pair = jax.random.randint(keys[6], (), 0, HIST - 1)
    strong = jnp.exp(jax.random.uniform(keys[7], (HIST - 1,), jnp.float32, math.log(0.6), math.log(3.0)))
    weak = jnp.exp(jax.random.uniform(keys[8], (HIST - 1,), jnp.float32, math.log(0.03), math.log(0.12)))
    kappa = jnp.where(jnp.arange(HIST - 1) == weak_pair, weak, strong)
    changes = kappa[:, None, None, None] * curve * steps_all[:HIST - 1]
    extra = jax.random.normal(keys[9], (2, OBJ, OBJ_ALL), jnp.float32)
    older = jnp.clip(TIKHONOV * base + scale * (pull[HIST - 1] * curve * base + 0.3 * extra), -40.0, 40.0)
    return (base, steps_all, changes, older)


def draw_transmission(key, part):
    return history(key)[0]


def draw_past_steps(key, part):
    return history(key)[1]


def draw_past_changes(key, part):
    return history(key)[2]


def draw_old_gradient(key, part):
    return history(key)[3]


def draw_positions(key, part):
    key_all, key_pick, key_other = jax.random.split(key, 3)
    spots = jax.random.randint(key_all, (FRAMES, 2), 0, SPAN + 1)
    first = jax.random.randint(key_pick, (), 0, FRAMES)
    second = jax.random.randint(key_other, (), 0, FRAMES)
    spots = spots.at[first, 0].set(SPAN)
    spots = spots.at[second, 1].set(0)
    return spots.astype(jnp.int32)


def block_levels(stream_key, dims, cuts, least, high):
    def one(axis_at, parts):
        steps = jax.random.uniform(jax.random.fold_in(jax.random.fold_in(stream_key, 6), axis_at), (parts,), jnp.float32, least / len(cuts), high / len(cuts))
        return jnp.repeat(jnp.exp(steps), dims[axis_at] // parts).reshape((-1,) + (1,) * (len(dims) - axis_at - 1))

    level = one(*cuts[0])
    for cut in cuts[1:]:
        level = level * one(*cut)
    return level


def bell_draw(key, extent, deviation, limit, cuts=(), kind=jnp.bfloat16):
    drawn = jax.random.normal(key, extent, jnp.float32) * deviation
    if len(cuts) > 0:
        drawn = block_levels(key, extent, cuts, -0.22, 0.18) * drawn
    return jnp.clip(drawn, min=-limit, max=limit).astype(kind)


def setup_inputs(seed: int = 0) -> dict:
    splits = jax.random.split(jax.random.key(seed), 8)
    transmission = draw_transmission(jax.random.fold_in(splits[7], 71), 0)
    probe = bell_draw(splits[1], (2, MODES, N, N), 0.25, 1.5, ((2, 16),))
    measured = jnp.clip(2.0 * jax.random.uniform(splits[2], (FRAMES, N, N), jnp.float32) ** block_levels(splits[2], (FRAMES, N, N), ((0, 32), (1, 16)), -0.2, 0.2), 0.0, 2.0)
    positions = draw_positions(jax.random.fold_in(splits[7], 71), 0)
    past_steps = draw_past_steps(jax.random.fold_in(splits[7], 71), 0)
    past_changes = draw_past_changes(jax.random.fold_in(splits[7], 71), 0)
    old_gradient = draw_old_gradient(jax.random.fold_in(splits[7], 71), 0)
    return dict(transmission=transmission, probe=probe, measured=measured, positions=positions, past_steps=past_steps, past_changes=past_changes, old_gradient=old_gradient)


TWO_PI = 2.0 * math.pi
CURVE_FLOOR = 0.25
TIKHONOV = 0.5
EPSILON = 1e-06

def dft_tables(count):
    index = jnp.arange(count, dtype=jnp.int32)
    phase = (index[:, None] * index[None, :] % count).astype(jnp.float32) * (TWO_PI / count)
    factor = 1.0 / math.sqrt(count)
    return ((jnp.cos(phase) * factor).astype(jnp.bfloat16), (-jnp.sin(phase) * factor).astype(jnp.bfloat16))

def chirp_table(count):
    index = jnp.arange(count, dtype=jnp.int32)
    wavenumber = (index + count // 2) % count - count // 2
    phase = (wavenumber * wavenumber % (4 * count)).astype(jnp.float32) * (TWO_PI / (4 * count))
    return (jnp.cos(phase), -jnp.sin(phase))

def rotate(real_part, imag_part, turn_real, turn_imag):
    return (real_part * turn_real - imag_part * turn_imag, real_part * turn_imag + imag_part * turn_real)

def narrow(pair):
    return jnp.stack([pair[0], pair[1]]).astype(jnp.bfloat16)

def right_product(field, matrix_real, matrix_imag):

    def single(left, right):
        return jnp.einsum('...k,kj->...j', left.astype(jnp.float32), right.astype(jnp.float32), precision=lax.Precision.HIGHEST)
    return (single(field[0], matrix_real) - single(field[1], matrix_imag), single(field[0], matrix_imag) + single(field[1], matrix_real))

def left_product(matrix_real, matrix_imag, field):

    def single(left, right):
        return jnp.einsum('jk,...kc->...jc', left.astype(jnp.float32), right.astype(jnp.float32), precision=lax.Precision.HIGHEST)
    return (single(matrix_real, field[0]) - single(matrix_imag, field[1]), single(matrix_real, field[1]) + single(matrix_imag, field[0]))

def inner(left, right):
    return jnp.sum(left * right)

def reference(transmission, probe, measured, positions, past_steps, past_changes, old_gradient):
    fwd_real, fwd_imag = dft_tables(N)
    inv_imag = -fwd_imag
    chirp_real, chirp_imag = chirp_table(N)
    tiles = transmission.astype(jnp.bfloat16).reshape(2, OBJ, N_REGION, OBJ)
    probe_wide = probe.astype(jnp.float32)
    anchor = jnp.zeros((), jnp.int32)

    def one_frame(total, inputs):
        target, offset, frame = inputs
        region = (frame // FR).astype(jnp.int32)
        corner = (anchor, offset[1].astype(jnp.int32), region, offset[0].astype(jnp.int32))
        window = jnp.swapaxes(lax.dynamic_slice(tiles, corner, (2, N, 1, N))[:, :, 0, :], 1, 2).astype(jnp.float32)
        wave = narrow(rotate(probe_wide[0], probe_wide[1], window[0], window[1]))
        section = narrow(rotate(*right_product(wave, fwd_real, fwd_imag), chirp_real, chirp_imag))
        spread = narrow(right_product(section, fwd_real, inv_imag))
        section = narrow(rotate(*left_product(fwd_real, fwd_imag, spread), chirp_real[:, None], chirp_imag[:, None]))
        far_field = narrow(left_product(fwd_real, inv_imag, section)).astype(jnp.float32)
        misfit = lax.optimization_barrier(jnp.sum(far_field[0] * far_field[0] + far_field[1] * far_field[1], axis=0)) - target
        weighted = (misfit * far_field).astype(jnp.bfloat16)
        section = narrow(rotate(*left_product(fwd_real, fwd_imag, weighted), chirp_real[:, None], -chirp_imag[:, None]))
        returned = narrow(left_product(fwd_real, inv_imag, section))
        section = narrow(rotate(*right_product(returned, fwd_real, fwd_imag), chirp_real, -chirp_imag))
        back_real, back_imag = right_product(section, fwd_real, inv_imag)
        grad_real = 4.0 * lax.optimization_barrier(jnp.sum(probe_wide[0] * back_real + probe_wide[1] * back_imag, axis=0))
        grad_imag = 4.0 * lax.optimization_barrier(jnp.sum(probe_wide[0] * back_imag - probe_wide[1] * back_real, axis=0))
        frame_grad = jnp.swapaxes(jnp.stack([grad_real, grad_imag]), 1, 2)
        before = lax.dynamic_slice(total, corner, (2, N, 1, N))
        total = lax.dynamic_update_slice(total, before + frame_grad[:, :, None, :], corner)
        return (total, None)
    frame_ids = jnp.arange(FRAMES, dtype=jnp.int32)
    total, leftover = lax.scan(one_frame, jnp.zeros((2, OBJ, N_REGION, OBJ), jnp.float32), (measured, positions, frame_ids))
    gradient = total.reshape(2, OBJ, OBJ_ALL) + TIKHONOV * transmission
    steps_list = [past_steps[index] for index in range(HIST)]
    changes = [past_changes[index] for index in range(HIST - 1)] + [gradient - old_gradient]
    weights = [1.0 / jnp.maximum(inner(steps_list[index], changes[index]), CURVE_FLOOR * inner(steps_list[index], steps_list[index])) for index in range(HIST)]
    direction = gradient
    alphas = [None] * HIST
    for index in reversed(range(HIST)):
        alphas[index] = weights[index] * inner(steps_list[index], direction)
        direction = direction - alphas[index] * changes[index]
    last = HIST - 1
    scale = jnp.maximum(inner(steps_list[last], changes[last]), CURVE_FLOOR * inner(steps_list[last], steps_list[last])) / (inner(changes[last], changes[last]) + EPSILON)
    direction = scale * direction
    for index in range(HIST):
        beta = weights[index] * inner(changes[index], direction)
        direction = direction + (alphas[index] - beta) * steps_list[index]
    return (transmission - direction, gradient)
```

```python
import functools

import jax
import jax.numpy as jnp
import ml_dtypes
import numpy as np
from jax import lax
from jax.experimental import pallas as pl
from jax.experimental.pallas import tpu as pltpu
from jax.sharding import PartitionSpec as P

CURVE_FLOOR = 0.25
TIKHONOV = 0.5
EPSILON = 1e-06
F32 = jnp.float32
BF16 = jnp.bfloat16
LANES = 128


def propagator(count):
    index = np.arange(count)
    phase = np.outer(index, index) % count * (2.0 * np.pi / count)
    factor = 1.0 / np.sqrt(count)
    real = (np.cos(phase) * factor).astype(np.float32).astype(ml_dtypes.bfloat16)
    imag = (-np.sin(phase) * factor).astype(np.float32).astype(ml_dtypes.bfloat16)
    table = real.astype(np.float64) + 1j * imag.astype(np.float64)
    wavenumber = (index + count // 2) % count - count // 2
    chirp = np.exp(-2j * np.pi * (wavenumber * wavenumber % (4 * count)) / (4 * count))
    folded = (table * chirp[None, :]) @ table.conj()
    return np.stack([folded.real, folded.imag]).astype(np.float32).astype(ml_dtypes.bfloat16)


def dot(left, right):
    return jnp.dot(left, right, preferred_element_type=F32)


def dot_t(left, right):
    return lax.dot_general(left, right, (((1,), (1,)), ((), ())), preferred_element_type=F32)


def iota(shape, dim):
    return lax.broadcasted_iota(jnp.int32, shape, dim)


def quad(parts):
    lane = iota(parts[0].shape, 1)
    low = lane % 128 < 64
    even = lane % 64 < 32
    roll = lambda x, s: pltpu.roll(x, s, 1)
    a0 = jnp.where(low, parts[0], roll(parts[2], 64))
    a2 = jnp.where(low, roll(parts[0], 64), parts[2])
    a1 = jnp.where(low, parts[1], roll(parts[3], 64))
    a3 = jnp.where(low, roll(parts[1], 64), parts[3])
    return [
        jnp.where(even, a0, roll(a1, 32)),
        jnp.where(even, roll(a0, 96), a1),
        jnp.where(even, a2, roll(a3, 32)),
        jnp.where(even, roll(a2, 96), a3),
    ]


def spread_sum(x):
    x = x + pltpu.roll(x, 64, 1)
    return x + pltpu.roll(x, 32, 1)


def barrier(axis, size, also=()):
    sem = pltpu.get_barrier_semaphore()
    total = 0
    for name, count in ((axis, size), *also):
        me = lax.axis_index(name)

        def signal(k, carry, name=name, count=count, me=me):
            pl.semaphore_signal(
                sem,
                inc=1,
                device_id={name: lax.rem(me + k, count)},
                device_id_type=pl.DeviceIdType.MESH,
            )
            return carry

        lax.fori_loop(1, count, signal, 0)
        total += count - 1
    pl.semaphore_wait(sem, total)


def exchange(axis, size, src, dst, send, recv):
    me = lax.axis_index(axis)

    def copy(peer, slot):
        return pltpu.make_async_remote_copy(
            src_ref=src(peer),
            dst_ref=dst(slot),
            send_sem=send.at[peer],
            recv_sem=recv.at[slot],
            device_id={axis: peer},
            device_id_type=pl.DeviceIdType.MESH,
        )

    def start():
        def one(k, carry):
            copy(lax.rem(me + k, size), me).start()
            return carry

        lax.fori_loop(1, size, one, 0)

    def wait_recv():
        def one(k, carry):
            peer = lax.rem(me + k, size)
            copy(peer, peer).wait_recv()
            return carry

        lax.fori_loop(1, size, one, 0)

    def wait_send():
        def one(k, carry):
            copy(lax.rem(me + k, size), me).wait_send()
            return carry

        lax.fori_loop(1, size, one, 0)

    return start, wait_recv, wait_send


def frame_kernel(
    grp,
    pos,
    trans_hbm,
    probe_hbm,
    meas_hbm,
    k_hbm,
    out_ref,
    trans,
    probe,
    meas,
    kmat,
    x_send,
    x_recv,
    m_send,
    m_recv,
    f_send,
    f_recv,
    b_send,
    b_recv,
    g_send,
    g_recv,
    select,
    target,
    field,
    tile,
    load_sem,
    send_sem,
    recv_sem,
):
    me = lax.axis_index("grp")
    cols, length = trans.shape[1], trans.shape[2]
    modes, rows, n = probe.shape[1], probe.shape[2], probe.shape[3]
    tiles = n // LANES
    halves = modes // 4
    loads = [
        pltpu.make_async_copy(src, dst, load_sem.at[i])
        for i, (src, dst) in enumerate(
            ((trans_hbm, trans), (meas_hbm, meas), (probe_hbm, probe), (k_hbm, kmat))
        )
    ]
    for load in loads:
        load.start()
    row0, col0 = pos[0, 0], pos[0, 1]
    mine = lambda size: pl.ds(pl.multiple_of(me * size, size), size)

    loads[0].wait()
    gap = jnp.zeros((LANES // 2 - cols, length), F32)
    block = jnp.concatenate([trans[0], gap, trans[1], gap], axis=0).astype(BF16)
    pick = iota((n, length), 1) == iota((n, length), 0) + row0
    x_send[...] = dot_t(pick.astype(F32).astype(BF16), block).astype(BF16)
    x_recv[me] = x_send[mine(rows), :]

    loads[1].wait()
    for t in range(tiles):
        packed = quad([meas[0, 8 * a : 8 * a + 8, LANES * t : LANES * (t + 1)] for a in range(4)])
        for g in range(4):
            m_send[4 * t + g] = packed[g]
    m_recv[me] = m_send[me]

    barrier("grp", grp)
    x_copy = exchange(
        "grp",
        grp,
        lambda p: x_send.at[pl.ds(pl.multiple_of(p * rows, rows), rows), :],
        lambda s: x_recv.at[s],
        send_sem.at[0],
        recv_sem.at[0],
    )
    m_copy = exchange(
        "grp", grp, lambda p: m_send.at[p], lambda s: m_recv.at[s], send_sem.at[1], recv_sem.at[1]
    )
    x_copy[0]()
    m_copy[0]()

    for d in range(grp):
        lane = iota((n, LANES), 1) % (LANES // 2)
        hit = (lane + cols * d == iota((n, LANES), 0) + col0) & (lane < cols)
        select[:, LANES * d : LANES * (d + 1)] = hit.astype(F32).astype(BF16)
    loads[2].wait()
    loads[3].wait()
    x_copy[1]()
    first = iota((rows, LANES), 1) < LANES // 2
    stacked = []
    for d in range(grp):
        x = x_recv[d].astype(F32)
        zero = jnp.zeros_like(x)
        stacked.append(
            jnp.concatenate([jnp.where(first, x, zero), jnp.where(first, zero, x), zero, zero], axis=0).astype(BF16)
        )
    window = jnp.transpose(dot_t(select[...], jnp.concatenate(stacked, axis=1)))
    win_r, win_i = window[:rows], window[rows : 2 * rows]

    k_r, k_i = kmat[0], kmat[1]
    f_copies, b_copies = [], []
    for q in range(halves):
        wave_r, wave_i = [], []
        for m in range(4 * q, 4 * q + 4):
            p_r, p_i = probe[0, m].astype(F32), probe[1, m].astype(F32)
            wave_r.append(p_r * win_r - p_i * win_i)
            wave_i.append(p_r * win_i + p_i * win_r)
        wave_r = jnp.concatenate(wave_r, axis=0).astype(BF16)
        wave_i = jnp.concatenate(wave_i, axis=0).astype(BF16)
        out = (
            dot(wave_r, k_r) - dot(wave_i, k_i),
            dot(wave_r, k_i) + dot(wave_i, k_r),
        )
        for c in range(2):
            for t in range(tiles):
                packed = quad(
                    [out[c][rows * m : rows * (m + 1), LANES * t : LANES * (t + 1)] for m in range(4)]
                )
                for g in range(4):
                    f_send[q, 4 * t + g, :, LANES * c : LANES * (c + 1)] = packed[g].astype(BF16)
        f_recv[q, me] = f_send[q, me]
        f_copies.append(
            exchange(
                "grp",
                grp,
                lambda p, q=q: f_send.at[q, p],
                lambda s, q=q: f_recv.at[q, s],
                send_sem.at[2 + q],
                recv_sem.at[2 + q],
            )
        )
        f_copies[q][0]()

    m_copy[1]()
    packed = m_recv[...].reshape(grp * 8, LANES)
    group = iota((grp * 8, LANES), 1) // 32
    for a in range(4):
        spread = spread_sum(jnp.where(group == a, packed, jnp.zeros_like(packed)))
        target[:, a] = spread.reshape(grp, 8, LANES)

    intensity = jnp.zeros((n, LANES), F32)
    for q in range(halves):
        f_copies[q][1]()
        x = f_recv[q].reshape(n, 2 * LANES)
        by_r, by_i = dot(k_r, x), dot(k_i, x)
        d_r = (by_r[:, :LANES] - by_i[:, LANES:]).astype(BF16)
        d_i = (by_r[:, LANES:] + by_i[:, :LANES]).astype(BF16)
        field[q, :, :LANES] = d_r
        field[q, :, LANES:] = d_i
        d_r, d_i = d_r.astype(F32), d_i.astype(F32)
        intensity = intensity + (d_r * d_r + d_i * d_i)
    misfit = spread_sum(intensity) - target[...].reshape(n, LANES)
    for q in range(halves):
        e_r = (misfit * field[q, :, :LANES].astype(F32)).astype(BF16)
        e_i = (misfit * field[q, :, LANES:].astype(F32)).astype(BF16)
        e = jnp.concatenate([e_r, e_i], axis=1)
        by_r, by_i = dot(k_r, e), dot(k_i, e)
        b_send[q, :, :, :LANES] = (by_r[:, :LANES] + by_i[:, LANES:]).astype(BF16).reshape(grp, rows, LANES)
        b_send[q, :, :, LANES:] = (by_r[:, LANES:] - by_i[:, :LANES]).astype(BF16).reshape(grp, rows, LANES)
        b_recv[q, me] = b_send[q, me]
        b_copies.append(
            exchange(
                "grp",
                grp,
                lambda p, q=q: b_send.at[q, p],
                lambda s, q=q: b_recv.at[q, s],
                send_sem.at[2 + halves + q],
                recv_sem.at[2 + halves + q],
            )
        )
        b_copies[q][0]()

    grad_r = jnp.zeros((rows, n), F32)
    grad_i = jnp.zeros((rows, n), F32)
    for q in range(halves):
        b_copies[q][1]()
        back = []
        for c in range(2):
            by_tile = []
            for t in range(tiles):
                packed = quad(
                    [b_recv[q, 4 * t + g, :, LANES * c : LANES * (c + 1)].astype(F32) for g in range(4)]
                )
                by_tile.append(jnp.concatenate(packed, axis=0))
            back.append(jnp.concatenate(by_tile, axis=1).astype(BF16))
        p_r = dot(back[0], k_r) + dot(back[1], k_i)
        p_i = dot(back[1], k_r) - dot(back[0], k_i)
        for m in range(4):
            w_r, w_i = probe[0, 4 * q + m].astype(F32), probe[1, 4 * q + m].astype(F32)
            o_r, o_i = p_r[rows * m : rows * (m + 1)], p_i[rows * m : rows * (m + 1)]
            grad_r = grad_r + (w_r * o_r + w_i * o_i)
            grad_i = grad_i + (w_r * o_i - w_i * o_r)

    grad_r = (4.0 * grad_r).astype(BF16)
    grad_i = (4.0 * grad_i).astype(BF16)
    place = iota((length, n), 0) == iota((length, n), 1) + col0
    tall = dot_t(
        place.astype(F32).astype(BF16), jnp.concatenate([grad_r] * 4 + [grad_i] * 4, axis=0)
    )
    tall = tall.reshape(grp, cols // 8, 8, 2 * LANES)
    parts = [
        tall[:, j, :, LANES * c : LANES * (c + 1)] for c in range(2) for j in range(cols // 8)
    ]
    group = iota((grp, 8, LANES), 2) // 32
    zero = jnp.zeros((grp, 8, LANES), F32)
    wide = []
    for w in range(4):
        value = zero
        for p in range(4):
            if 4 * w + p < len(parts):
                value = jnp.where(group == p, parts[4 * w + p], value)
        wide.append(value)
    g_send[...] = jnp.concatenate(wide, axis=1).astype(BF16)
    g_recv[me] = g_send[me]
    g_copy = exchange(
        "grp",
        grp,
        lambda p: g_send.at[p],
        lambda s: g_recv.at[s],
        send_sem.at[2 + 2 * halves],
        recv_sem.at[2 + 2 * halves],
    )
    g_copy[0]()
    put = (iota((n, length), 1) == iota((n, length), 0) + row0).astype(F32).astype(BF16)
    g_copy[1]()
    for t in range(tiles):
        whole = [g_recv[4 * t + g].astype(F32) for g in range(4)]
        for w in range((len(parts) + 3) // 4):
            packed = quad([x[8 * w : 8 * w + 8] for x in whole])
            for p in range(4):
                if 4 * w + p < len(parts):
                    at = 8 * (4 * w + p)
                    tile[at : at + 8, LANES * t : LANES * (t + 1)] = packed[p]
    out = dot(tile[...].astype(BF16), put)
    out_ref[0] = out[:cols]
    out_ref[1] = out[cols:]

    for copies in (x_copy, m_copy, *f_copies, *b_copies, g_copy):
        copies[2]()


def update_kernel(
    grp,
    region,
    data_ref,
    trans_ref,
    steps_ref,
    changes_ref,
    old_ref,
    updated_ref,
    gradient_ref,
    change,
    gram,
    one_send,
    one_recv,
    two_recv,
    one_send_sem,
    one_recv_sem,
    two_send_sem,
    two_recv_sem,
):
    depth = steps_ref.shape[0]
    last = depth - 1
    cols, length = trans_ref.shape[1], trans_ref.shape[2]
    strips = [(c, j) for c in range(2) for j in range(cols // 8)]
    names = []
    for i in range(depth):
        names += [("ss", i, i), ("sg", i, i), ("yg", i, i)]
        for j in range(i, depth):
            names += [("sy", i, j), ("yy", i, j)]
    slot = {name: number for number, name in enumerate(names)}
    gram[...] = jnp.zeros_like(gram)
    for c, j in strips:
        at = (c, slice(8 * j, 8 * j + 8), slice(None))
        grad = data_ref[at] + TIKHONOV * trans_ref[at]
        gradient_ref[at] = grad
        new = grad - old_ref[at]
        change[at] = new
        s = [steps_ref[(i, *at)] for i in range(depth)]
        y = [changes_ref[(i, *at)] for i in range(depth - 1)] + [new]
        for (kind, a, b), number in slot.items():
            left = {"ss": s, "sg": s, "yg": y, "sy": s, "yy": y}[kind][a]
            right = {"ss": s, "sg": [grad] * depth, "yg": [grad] * depth, "sy": y, "yy": y}[kind][b]
            product = left * right
            gram[number] += sum(product[:, LANES * t : LANES * (t + 1)] for t in range(length // LANES))
    totals = jnp.sum(jnp.sum(gram[...], axis=1), axis=1, keepdims=True)
    group = iota((8, LANES), 1) // 32
    value = jnp.zeros((8, LANES), F32)
    for w in range(4):
        value = jnp.where(group == w, totals[8 * w : 8 * w + 8], value)
    one_send[0] = value

    barrier("grp", grp, (("region", region),))
    me, here = lax.axis_index("grp"), lax.axis_index("region")
    one_recv[me] = value
    one = exchange(
        "grp", grp, lambda p: one_send.at[0], lambda s: one_recv.at[s], one_send_sem, one_recv_sem
    )
    one[0]()
    one[1]()
    value = jnp.sum(one_recv[...], axis=0)
    one_send[1] = value
    two_recv[here] = value
    two = exchange(
        "region", region, lambda p: one_send.at[1], lambda s: two_recv.at[s], two_send_sem, two_recv_sem
    )
    two[0]()
    two[1]()
    value = jnp.sum(two_recv[...], axis=0)

    def inner(kind, a, b):
        number = slot[(kind, a, b)]
        at = 32 * (number // 8)
        return value[number % 8 : number % 8 + 1, at : at + 1]

    curve = [
        jnp.maximum(inner("sy", i, i), CURVE_FLOOR * inner("ss", i, i)) for i in range(depth)
    ]
    alphas = [None] * depth
    for i in reversed(range(depth)):
        along = inner("sg", i, i)
        for j in range(i + 1, depth):
            along = along - alphas[j] * inner("sy", i, j)
        alphas[i] = along / curve[i]
    scale = curve[last] / (inner("yy", last, last) + EPSILON)
    weights = []
    for i in range(depth):
        along = inner("yg", i, i)
        for j in range(depth):
            along = along - alphas[j] * inner("yy", min(i, j), max(i, j))
        along = scale * along
        for j in range(i):
            along = along + weights[j] * inner("sy", j, i)
        weights.append(alphas[i] - along / curve[i])
    alphas = [scale * alpha for alpha in alphas]
    for c, j in strips:
        at = (c, slice(8 * j, 8 * j + 8), slice(None))
        direction = scale * gradient_ref[at]
        for i in range(depth):
            y = change[at] if i == last else changes_ref[(i, *at)]
            direction = direction - alphas[i] * y + weights[i] * steps_ref[(i, *at)]
        updated_ref[at] = trans_ref[at] - direction
    one[2]()
    two[2]()


def shards(grp, region, transmission, probe, measured, positions, past_steps, past_changes, old_gradient):
    two, cols, length = transmission.shape
    _, modes, rows, n = probe.shape
    halves = modes // 4
    depth = past_steps.shape[0]
    phases = 3 + 2 * halves
    vmem = pl.BlockSpec(memory_space=pltpu.VMEM)
    hbm = pl.BlockSpec(memory_space=pl.ANY)
    data = pl.pallas_call(
        functools.partial(frame_kernel, grp),
        out_shape=jax.ShapeDtypeStruct((two, cols, length), F32),
        in_specs=[pl.BlockSpec(memory_space=pltpu.SMEM), hbm, hbm, hbm, hbm],
        out_specs=vmem,
        scratch_shapes=[
            pltpu.VMEM((two, cols, length), F32),
            pltpu.VMEM(probe.shape, BF16),
            pltpu.VMEM((1, rows, n), F32),
            pltpu.VMEM((2, n, n), BF16),
            pltpu.VMEM((n, LANES), BF16),
            pltpu.VMEM((grp, rows, LANES), BF16),
            pltpu.VMEM((grp, 8, LANES), F32),
            pltpu.VMEM((grp, 8, LANES), F32),
            pltpu.VMEM((halves, grp, rows, 2 * LANES), BF16),
            pltpu.VMEM((halves, grp, rows, 2 * LANES), BF16),
            pltpu.VMEM((halves, grp, rows, 2 * LANES), BF16),
            pltpu.VMEM((halves, grp, rows, 2 * LANES), BF16),
            pltpu.VMEM((grp, 32, LANES), BF16),
            pltpu.VMEM((grp, 32, LANES), BF16),
            pltpu.VMEM((n, grp * LANES), BF16),
            pltpu.VMEM((grp, 4, 8, LANES), F32),
            pltpu.VMEM((halves, n, 2 * LANES), BF16),
            pltpu.VMEM((two * cols, n), F32),
            pltpu.SemaphoreType.DMA((4,)),
            pltpu.SemaphoreType.DMA((phases, grp)),
            pltpu.SemaphoreType.DMA((phases, grp)),
        ],
        compiler_params=pltpu.CompilerParams(
            collective_id=0, has_side_effects=True, vmem_limit_bytes=48 << 20
        ),
        name="frame",
    )(positions, transmission, probe, measured, jnp.asarray(propagator(n)))
    shape = jax.ShapeDtypeStruct((two, cols, length), F32)
    return pl.pallas_call(
        functools.partial(update_kernel, grp, region),
        out_shape=(shape, shape),
        in_specs=[vmem] * 5,
        out_specs=(vmem, vmem),
        scratch_shapes=[
            pltpu.VMEM((two, cols, length), F32),
            pltpu.VMEM((32, 8, LANES), F32),
            pltpu.VMEM((2, 8, LANES), F32),
            pltpu.VMEM((grp, 8, LANES), F32),
            pltpu.VMEM((region, 8, LANES), F32),
            pltpu.SemaphoreType.DMA((grp,)),
            pltpu.SemaphoreType.DMA((grp,)),
            pltpu.SemaphoreType.DMA((region,)),
            pltpu.SemaphoreType.DMA((region,)),
        ],
        compiler_params=pltpu.CompilerParams(
            collective_id=1, has_side_effects=True, vmem_limit_bytes=32 << 20
        ),
        name="update",
    )(data, transmission, past_steps, past_changes, old_gradient)


def solution(mesh):
    return jax.shard_map(
        functools.partial(shards, mesh.shape["grp"], mesh.shape["region"]),
        mesh=mesh,
        in_specs=(
            P(None, "grp", "region"),
            P(None, None, "grp", None),
            P("region", "grp", None),
            P("region", None),
            P(None, None, "grp", "region"),
            P(None, None, "grp", "region"),
            P(None, "grp", "region"),
        ),
        out_specs=(P(None, "grp", "region"), P(None, "grp", "region")),
        check_vma=False,
    )
```

```python
import functools

import jax
import jax.numpy as jnp
import ml_dtypes
import numpy as np
from jax import lax
from jax.experimental import pallas as pl
from jax.experimental.pallas import tpu as pltpu
from jax.sharding import PartitionSpec as P

CURVE_FLOOR = 0.25
TIKHONOV = 0.5
EPSILON = 1e-06
F32 = jnp.float32
BF16 = jnp.bfloat16
LANES = 128


def propagator(count):
    index = np.arange(count)
    phase = np.outer(index, index) % count * (2.0 * np.pi / count)
    factor = 1.0 / np.sqrt(count)
    real = (np.cos(phase) * factor).astype(np.float32).astype(ml_dtypes.bfloat16)
    imag = (-np.sin(phase) * factor).astype(np.float32).astype(ml_dtypes.bfloat16)
    table = real.astype(np.float64) + 1j * imag.astype(np.float64)
    wavenumber = (index + count // 2) % count - count // 2
    chirp = np.exp(-2j * np.pi * (wavenumber * wavenumber % (4 * count)) / (4 * count))
    folded = (table * chirp[None, :]) @ table.conj()
    return np.stack([folded.real, folded.imag]).astype(np.float32).astype(ml_dtypes.bfloat16)


def dot(left, right):
    return jnp.dot(left, right, preferred_element_type=F32)


def dot_t(left, right):
    return lax.dot_general(left, right, (((1,), (1,)), ((), ())), preferred_element_type=F32)


def iota(shape, dim):
    return lax.broadcasted_iota(jnp.int32, shape, dim)


def swap(parts):
    count = len(parts)
    width = LANES // count
    lane = iota(parts[0].shape, 1)
    step = count // 2
    while step:
        low = lane % (2 * step * width) < step * width
        out = list(parts)
        for i in range(count):
            if i & step == 0:
                a, b = parts[i], parts[i + step]
                out[i] = jnp.where(low, a, pltpu.roll(b, step * width, 1))
                out[i + step] = jnp.where(low, pltpu.roll(a, LANES - step * width, 1), b)
        parts = out
        step //= 2
    return parts


def spread_sum(x, width):
    step = LANES // 2
    while step >= width:
        x = x + pltpu.roll(x, step, 1)
        step //= 2
    return x


class Exchange:
    def __init__(self, axis, size, src, dst, send, recv):
        self.axis, self.size, self.src, self.dst, self.send, self.recv = axis, size, src, dst, send, recv
        self.me = lax.axis_index(axis)

    def copy(self, peer, slot):
        return pltpu.make_async_remote_copy(
            src_ref=self.src(peer),
            dst_ref=self.dst(slot),
            send_sem=self.send.at[peer],
            recv_sem=self.recv.at[slot],
            device_id={self.axis: peer},
            device_id_type=pl.DeviceIdType.MESH,
        )

    def each(self, act):
        def one(k, carry):
            act(lax.rem(self.me + k, self.size))
            return carry

        lax.fori_loop(1, self.size, one, 0)

    def start(self):
        self.each(lambda peer: self.copy(peer, self.me).start())

    def wait_recv(self):
        self.each(lambda peer: self.copy(peer, peer).wait_recv())

    def wait_send(self):
        self.each(lambda peer: self.copy(peer, self.me).wait_send())


def signal_all(axes):
    sem = pltpu.get_barrier_semaphore()
    for name, count in axes:
        me = lax.axis_index(name)

        def signal(k, carry, name=name, count=count, me=me):
            pl.semaphore_signal(
                sem,
                inc=1,
                device_id={name: lax.rem(me + k, count)},
                device_id_type=pl.DeviceIdType.MESH,
            )
            return carry

        lax.fori_loop(1, count, signal, 0)


def wait_all(axes):
    pl.semaphore_wait(pltpu.get_barrier_semaphore(), sum(count - 1 for _, count in axes))


def step_kernel(
    grp,
    region,
    pos,
    trans_hbm,
    meas_hbm,
    probe_hbm,
    k_hbm,
    steps_hbm,
    changes_hbm,
    old_hbm,
    data_ref,
    direction_ref,
    trans,
    meas,
    probe,
    kmat,
    steps,
    changes,
    old,
    x_send,
    x_recv,
    m_send,
    m_recv,
    f_send,
    f_recv,
    b_send,
    b_recv,
    g_send,
    g_recv,
    one_send,
    one_recv,
    two_recv,
    select,
    wave,
    target,
    back_r,
    back_i,
    tile,
    gram,
    gradient,
    change,
    load_sem,
    send_sem,
    recv_sem,
    two_send_sem,
    two_recv_sem,
):
    me, here = lax.axis_index("grp"), lax.axis_index("region")
    axes = (("grp", grp), ("region", region))
    cols, length = trans.shape[1], trans.shape[2]
    modes, rows, n = probe.shape[1], probe.shape[2], probe.shape[3]
    tiles = n // LANES
    parts = 2
    width = n // (grp * parts)
    per_part = tiles // parts
    part = n // parts
    depth = steps.shape[0]
    last = depth - 1
    signal_all(axes)
    loads = [
        pltpu.make_async_copy(src, dst, load_sem.at[i])
        for i, (src, dst) in enumerate(
            (
                (trans_hbm, trans),
                (meas_hbm, meas),
                (probe_hbm, probe),
                (k_hbm, kmat),
                (steps_hbm, steps),
                (changes_hbm, changes),
                (old_hbm, old),
            )
        )
    ]
    for load in loads:
        load.start()
    row0, col0 = pos[0, 0], pos[0, 1]
    mine = pl.ds(pl.multiple_of(me * rows, rows), rows)
    phase = [0]
    copies = []

    def exchange(src, dst):
        at = phase[0]
        phase[0] += 1
        copies.append(Exchange("grp", grp, src, dst, send_sem.at[at], recv_sem.at[at]))
        return copies[-1]

    loads[0].wait()
    gap = jnp.zeros((LANES // 2 - cols, length), F32)
    block = jnp.concatenate([trans[0], gap, trans[1], gap], axis=0).astype(BF16)
    pick = iota((n, length), 1) == iota((n, length), 0) + row0
    x_send[...] = dot_t(pick.astype(F32).astype(BF16), block).astype(BF16)
    x_recv[me] = x_send[mine, :]
    wait_all(axes)
    x_copy = exchange(
        lambda p: x_send.at[pl.ds(pl.multiple_of(p * rows, rows), rows), :], lambda s: x_recv.at[s]
    )
    x_copy.start()

    loads[1].wait()
    for t in range(per_part):
        packed = swap(
            [
                meas[0, 8 * a : 8 * a + 8, LANES * (per_part * h + t) : LANES * (per_part * h + t + 1)]
                for h in range(parts)
                for a in range(rows // 8)
            ]
        )
        for g in range(8):
            m_send[8 * t + g] = packed[g]
    m_recv[me] = m_send[me]
    m_copy = exchange(lambda p: m_send.at[p], lambda s: m_recv.at[s])
    m_copy.start()

    for d in range(grp):
        lane = iota((n, LANES), 1) % (LANES // 2)
        hit = (lane + cols * d == iota((n, LANES), 0) + col0) & (lane < cols)
        select[:, LANES * d : LANES * (d + 1)] = hit.astype(F32).astype(BF16)
    loads[2].wait()
    loads[3].wait()
    x_copy.wait_recv()
    first = iota((rows, LANES), 1) < LANES // 2
    stacked = []
    for d in range(grp):
        x = x_recv[d].astype(F32)
        zero = jnp.zeros_like(x)
        stacked.append(
            jnp.concatenate([jnp.where(first, x, zero), jnp.where(first, zero, x), zero, zero], axis=0).astype(BF16)
        )
    window = jnp.transpose(dot_t(select[...], jnp.concatenate(stacked, axis=1)))
    win_r, win_i = window[:rows], window[rows : 2 * rows]
    for m in range(modes):
        p_r, p_i = probe[0, m].astype(F32), probe[1, m].astype(F32)
        wave[0, rows * m : rows * (m + 1)] = (p_r * win_r - p_i * win_i).astype(BF16)
        wave[1, rows * m : rows * (m + 1)] = (p_r * win_i + p_i * win_r).astype(BF16)

    f_copies, b_copies = [], []
    for q in range(parts):
        span = slice(part * q, part * (q + 1))
        k_r, k_i = kmat[0, :, span], kmat[1, :, span]
        out = (
            dot(wave[0], k_r) - dot(wave[1], k_i),
            dot(wave[0], k_i) + dot(wave[1], k_r),
        )
        for c in range(2):
            for t in range(per_part):
                packed = swap(
                    [out[c][rows * m : rows * (m + 1), LANES * t : LANES * (t + 1)] for m in range(modes)]
                )
                for g in range(8):
                    f_send[q, 8 * t + g, :, LANES * c : LANES * (c + 1)] = packed[g].astype(BF16)
        f_recv[q, me] = f_send[q, me]
        f_copies.append(exchange(lambda p, q=q: f_send.at[q, p], lambda s, q=q: f_recv.at[q, s]))
        f_copies[q].start()

    m_copy.wait_recv()
    packed = m_recv[...].reshape(grp * 8, LANES)
    group = iota((grp * 8, LANES), 1) // width
    for h in range(parts):
        for a in range(rows // 8):
            hit = group == h * (rows // 8) + a
            spread = spread_sum(jnp.where(hit, packed, jnp.zeros_like(packed)), width)
            target[h, :, a] = spread.reshape(grp, 8, LANES)

    for load in loads[4:]:
        load.wait()
    spots = [
        (c, slice(8 * j, 8 * j + 8), slice(LANES * t, LANES * (t + 1)))
        for c in range(2)
        for j in range(cols // 8)
        for t in range(length // LANES)
    ]
    early, late = [], []
    for i in range(depth):
        early.append(("ss", i, i))
        late += [("sg", i, i), ("yg", i, i), ("sy", i, last), ("yy", i, last)]
        for j in range(i, last):
            early += [("sy", i, j), ("yy", i, j)]
    number = {name: at for at, name in enumerate(early + late)}

    def accumulate(names, vectors):
        sums = [None] * len(names)
        for at in spots:
            value = vectors(at)
            for e, (kind, a, b) in enumerate(names):
                left = value[kind[0]][a]
                right = value["g"] if kind[1] == "g" else value[kind[1]][b]
                sums[e] = left * right if sums[e] is None else sums[e] + left * right
        for name, total in zip(names, sums):
            gram[number[name] : number[name] + 1, :] = jnp.sum(total, axis=0, keepdims=True)

    def known(at):
        return {
            "s": [steps[(i, *at)] for i in range(depth)],
            "y": [changes[(i, *at)] for i in range(last)],
        }

    accumulate(early, known)

    for q in range(parts):
        f_copies[q].wait_recv()
        x = f_recv[q].reshape(n, 2 * LANES)
        by_r, by_i = dot(kmat[0], x), dot(kmat[1], x)
        d_r = (by_r[:, :LANES] - by_i[:, LANES:]).astype(BF16).astype(F32)
        d_i = (by_r[:, LANES:] + by_i[:, :LANES]).astype(BF16).astype(F32)
        misfit = spread_sum(d_r * d_r + d_i * d_i, width) - target[q].reshape(n, LANES)
        e = jnp.concatenate([(misfit * d_r).astype(BF16), (misfit * d_i).astype(BF16)], axis=1)
        by_r, by_i = dot(kmat[0], e), dot(kmat[1], e)
        b_send[q, :, :, :LANES] = (by_r[:, :LANES] + by_i[:, LANES:]).astype(BF16).reshape(grp, rows, LANES)
        b_send[q, :, :, LANES:] = (by_r[:, LANES:] - by_i[:, :LANES]).astype(BF16).reshape(grp, rows, LANES)
        b_recv[q, me] = b_send[q, me]
        b_copies.append(exchange(lambda p, q=q: b_send.at[q, p], lambda s, q=q: b_recv.at[q, s]))
        b_copies[q].start()

    for q in range(parts):
        b_copies[q].wait_recv()
        back = []
        for c in range(2):
            by_tile = []
            for t in range(per_part):
                packed = swap(
                    [b_recv[q, 8 * t + g, :, LANES * c : LANES * (c + 1)].astype(F32) for g in range(8)]
                )
                by_tile.append(jnp.concatenate(packed, axis=0))
            back.append(jnp.concatenate(by_tile, axis=1).astype(BF16))
        span = slice(part * q, part * (q + 1))
        k_r, k_i = kmat[0, span, :], kmat[1, span, :]
        p_r = dot(back[0], k_r) + dot(back[1], k_i)
        p_i = dot(back[1], k_r) - dot(back[0], k_i)
        if q == 0:
            back_r[...] = p_r
            back_i[...] = p_i
        else:
            back_r[...] += p_r
            back_i[...] += p_i
    grad_r = jnp.zeros((rows, n), F32)
    grad_i = jnp.zeros((rows, n), F32)
    for m in range(modes):
        w_r, w_i = probe[0, m].astype(F32), probe[1, m].astype(F32)
        o_r, o_i = back_r[rows * m : rows * (m + 1)], back_i[rows * m : rows * (m + 1)]
        grad_r = grad_r + (w_r * o_r + w_i * o_i)
        grad_i = grad_i + (w_r * o_i - w_i * o_r)

    grad_r = (4.0 * grad_r).astype(BF16)
    grad_i = (4.0 * grad_i).astype(BF16)
    place = iota((length, n), 0) == iota((length, n), 1) + col0
    tall = dot_t(
        place.astype(F32).astype(BF16), jnp.concatenate([grad_r] * 4 + [grad_i] * 4, axis=0)
    )
    tall = tall.reshape(grp, cols // 8, 8, 2 * LANES)
    pieces = [
        tall[:, j, :, LANES * c : LANES * (c + 1)] for c in range(2) for j in range(cols // 8)
    ]
    group = iota((grp, 8, LANES), 2) // 32
    zero = jnp.zeros((grp, 8, LANES), F32)
    wide = []
    for w in range(4):
        value = zero
        for p in range(4):
            if 4 * w + p < len(pieces):
                value = jnp.where(group == p, pieces[4 * w + p], value)
        wide.append(value)
    g_send[...] = jnp.concatenate(wide, axis=1).astype(BF16)
    g_recv[me] = g_send[me]
    g_copy = exchange(lambda p: g_send.at[p], lambda s: g_recv.at[s])
    g_copy.start()
    put = (iota((n, length), 1) == iota((n, length), 0) + row0).astype(F32).astype(BF16)
    g_copy.wait_recv()
    for t in range(tiles):
        whole = [g_recv[4 * t + g].astype(F32) for g in range(4)]
        for w in range((len(pieces) + 3) // 4):
            packed = swap([x[8 * w : 8 * w + 8] for x in whole])
            for p in range(4):
                if 4 * w + p < len(pieces):
                    at = 8 * (4 * w + p)
                    tile[at : at + 8, LANES * t : LANES * (t + 1)] = packed[p]
    out = dot(tile[...].astype(BF16), put)
    data_ref[0] = out[:cols]
    data_ref[1] = out[cols:]

    def fresh(at):
        grad = data_ref[at] + TIKHONOV * trans[at]
        new = grad - old[at]
        gradient[at] = grad
        change[at] = new
        value = known(at)
        value["y"].append(new)
        value["g"] = grad
        return value

    accumulate(late, fresh)
    totals = jnp.sum(gram[...], axis=1, keepdims=True)
    count = gram.shape[0]
    totals = jnp.where(
        iota((count, LANES), 0) == iota((count, LANES), 1), totals, jnp.zeros((count, LANES), F32)
    )
    value = jnp.sum(totals, axis=0, keepdims=True)
    one_send[0] = value
    one_recv[me] = value
    one = exchange(lambda p: one_send.at[0], lambda s: one_recv.at[s])
    one.start()
    one.wait_recv()
    value = jnp.sum(one_recv[...], axis=0)
    one_send[1] = value
    two_recv[here] = value
    two = Exchange(
        "region", region, lambda p: one_send.at[1], lambda s: two_recv.at[s], two_send_sem, two_recv_sem
    )
    two.start()
    two.wait_recv()
    value = jnp.sum(two_recv[...], axis=0)

    def inner(kind, a, b):
        at = number[(kind, a, b)]
        return value[:, at : at + 1]

    curve = [
        jnp.maximum(inner("sy", i, i), CURVE_FLOOR * inner("ss", i, i)) for i in range(depth)
    ]
    alphas = [None] * depth
    for i in reversed(range(depth)):
        along = inner("sg", i, i)
        for j in range(i + 1, depth):
            along = along - alphas[j] * inner("sy", i, j)
        alphas[i] = along / curve[i]
    scale = curve[last] / (inner("yy", last, last) + EPSILON)
    weights = []
    for i in range(depth):
        along = inner("yg", i, i)
        for j in range(depth):
            along = along - alphas[j] * inner("yy", min(i, j), max(i, j))
        along = scale * along
        for j in range(i):
            along = along + weights[j] * inner("sy", j, i)
        weights.append(alphas[i] - along / curve[i])
    wide = lambda x: jnp.broadcast_to(x, (8, LANES))
    alphas = [wide(scale * alpha) for alpha in alphas]
    weights = [wide(weight) for weight in weights]
    scale = wide(scale)
    for at in spots:
        direction = scale * gradient[at]
        for i in range(depth):
            y = change[at] if i == last else changes[(i, *at)]
            direction = direction - alphas[i] * y + weights[i] * steps[(i, *at)]
        direction_ref[at] = direction
    for copy in (*copies, two):
        copy.wait_send()


def shards(grp, region, transmission, probe, measured, positions, past_steps, past_changes, old_gradient):
    two, cols, length = transmission.shape
    _, modes, rows, n = probe.shape
    parts = 2
    phases = 4 + 2 * parts
    vmem = pl.BlockSpec(memory_space=pltpu.VMEM)
    hbm = pl.BlockSpec(memory_space=pltpu.HBM)
    shape = jax.ShapeDtypeStruct((two, cols, length), F32)
    block = (parts, grp, rows, 2 * LANES)
    data, direction = pl.pallas_call(
        functools.partial(step_kernel, grp, region),
        out_shape=(shape, shape),
        in_specs=[pl.BlockSpec(memory_space=pltpu.SMEM)] + [hbm] * 7,
        out_specs=(vmem, vmem),
        scratch_shapes=[
            pltpu.VMEM((two, cols, length), F32),
            pltpu.VMEM(measured.shape, F32),
            pltpu.VMEM(probe.shape, BF16),
            pltpu.VMEM((2, n, n), BF16),
            pltpu.VMEM(past_steps.shape, F32),
            pltpu.VMEM(past_changes.shape, F32),
            pltpu.VMEM((two, cols, length), F32),
            pltpu.VMEM((n, LANES), BF16),
            pltpu.VMEM((grp, rows, LANES), BF16),
            pltpu.VMEM((grp, 8, LANES), F32),
            pltpu.VMEM((grp, 8, LANES), F32),
            pltpu.VMEM(block, BF16),
            pltpu.VMEM(block, BF16),
            pltpu.VMEM(block, BF16),
            pltpu.VMEM(block, BF16),
            pltpu.VMEM((grp, 32, LANES), BF16),
            pltpu.VMEM((grp, 32, LANES), BF16),
            pltpu.VMEM((2, 1, LANES), F32),
            pltpu.VMEM((grp, 1, LANES), F32),
            pltpu.VMEM((region, 1, LANES), F32),
            pltpu.VMEM((n, grp * LANES), BF16),
            pltpu.VMEM((2, modes * rows, n), BF16),
            pltpu.VMEM((parts, grp, rows // 8, 8, LANES), F32),
            pltpu.VMEM((modes * rows, n), F32),
            pltpu.VMEM((modes * rows, n), F32),
            pltpu.VMEM((two * cols, n), F32),
            pltpu.VMEM((32, LANES), F32),
            pltpu.VMEM((two, cols, length), F32),
            pltpu.VMEM((two, cols, length), F32),
            pltpu.SemaphoreType.DMA((7,)),
            pltpu.SemaphoreType.DMA((phases, grp)),
            pltpu.SemaphoreType.DMA((phases, grp)),
            pltpu.SemaphoreType.DMA((region,)),
            pltpu.SemaphoreType.DMA((region,)),
        ],
        compiler_params=pltpu.CompilerParams(
            collective_id=0, has_side_effects=True, vmem_limit_bytes=58 << 20
        ),
        name="step",
    )(
        positions,
        transmission,
        measured,
        probe,
        jnp.asarray(propagator(n)),
        past_steps,
        past_changes,
        old_gradient,
    )
    return transmission - direction, data + TIKHONOV * transmission


def solution(mesh):
    return jax.shard_map(
        functools.partial(shards, mesh.shape["grp"], mesh.shape["region"]),
        mesh=mesh,
        in_specs=(
            P(None, "grp", "region"),
            P(None, None, "grp", None),
            P("region", "grp", None),
            P("region", None),
            P(None, None, "grp", "region"),
            P(None, None, "grp", "region"),
            P(None, "grp", "region"),
        ),
        out_specs=(P(None, "grp", "region"), P(None, "grp", "region")),
        check_vma=False,
    )
```

```python
import functools
import itertools

import jax
import jax.numpy as jnp
import ml_dtypes
import numpy as np
from jax import lax
from jax.experimental import pallas as pl
from jax.experimental.pallas import tpu as pltpu
from jax.sharding import PartitionSpec as P

CURVE_FLOOR = 0.25
TIKHONOV = 0.5
EPSILON = 1e-06
F32 = jnp.float32
BF16 = jnp.bfloat16
LANES = 128


def propagator(count):
    index = np.arange(count)
    phase = np.outer(index, index) % count * (2.0 * np.pi / count)
    factor = 1.0 / np.sqrt(count)
    real = (np.cos(phase) * factor).astype(np.float32).astype(ml_dtypes.bfloat16)
    imag = (-np.sin(phase) * factor).astype(np.float32).astype(ml_dtypes.bfloat16)
    table = real.astype(np.float64) + 1j * imag.astype(np.float64)
    wavenumber = (index + count // 2) % count - count // 2
    chirp = np.exp(-2j * np.pi * (wavenumber * wavenumber % (4 * count)) / (4 * count))
    folded = (table * chirp[None, :]) @ table.conj()
    return np.stack([folded.real, folded.imag]).astype(np.float32).astype(ml_dtypes.bfloat16)


def dot(left, right):
    return jnp.dot(left, right, preferred_element_type=F32)


def dot_t(left, right):
    return lax.dot_general(left, right, (((1,), (1,)), ((), ())), preferred_element_type=F32)


def iota(shape, dim):
    return lax.broadcasted_iota(jnp.int32, shape, dim)


def swap(parts):
    count = len(parts)
    width = LANES // count
    lane = iota(parts[0].shape, 1)
    step = count // 2
    while step:
        low = lane % (2 * step * width) < step * width
        out = list(parts)
        for i in range(count):
            if i & step == 0:
                a, b = parts[i], parts[i + step]
                out[i] = jnp.where(low, a, pltpu.roll(b, step * width, 1))
                out[i + step] = jnp.where(low, pltpu.roll(a, LANES - step * width, 1), b)
        parts = out
        step //= 2
    return parts


def spread_sum(x, width):
    step = LANES // 2
    while step >= width:
        x = x + pltpu.roll(x, step, 1)
        step //= 2
    return x


LAYOUT = {"grp": ((8, 1), (2, 2)), "region": ((8, 1), (2, 1), (2, 0.25))}


def hops(axis, offset):
    return sum(min(o, size - o) * far for o, (size, far) in zip(offset, LAYOUT[axis]))


ORDER = {
    axis: sorted(
        (offset for offset in itertools.product(*(range(size) for size, _ in layout)) if any(offset)),
        key=lambda offset, axis=axis: -hops(axis, offset),
    )
    for axis, layout in LAYOUT.items()
}


def peers(axis):
    me = lax.axis_index(axis)
    digits, unit = [], 1
    for size, _ in reversed(LAYOUT[axis]):
        digits.insert(0, lax.rem(lax.div(me, unit), size))
        unit *= size
    found = []
    for offset in ORDER[axis]:
        peer = 0
        for o, digit, (size, _) in zip(offset, digits, LAYOUT[axis]):
            peer = peer * size + (lax.rem(digit + o, size) if o else digit)
        found.append(peer)
    return found


class Exchange:
    def __init__(self, axis, others, src, dst, send, recv):
        self.axis, self.others, self.src, self.dst, self.send, self.recv = axis, others, src, dst, send, recv
        self.me = lax.axis_index(axis)

    def copy(self, peer, slot):
        return pltpu.make_async_remote_copy(
            src_ref=self.src(peer),
            dst_ref=self.dst(slot),
            send_sem=self.send.at[peer],
            recv_sem=self.recv.at[slot],
            device_id={self.axis: peer},
            device_id_type=pl.DeviceIdType.MESH,
        )

    def each(self, act):
        for peer in self.others:
            act(peer)

    def start(self):
        self.each(lambda peer: self.copy(peer, self.me).start())

    def wait_recv(self):
        self.each(lambda peer: self.copy(peer, peer).wait_recv())

    def wait_send(self):
        self.each(lambda peer: self.copy(peer, self.me).wait_send())


def signal_all(others):
    sem = pltpu.get_barrier_semaphore()
    order = [
        (hops(axis, offset), axis, peer)
        for axis, members in others.items()
        for offset, peer in zip(ORDER[axis], members)
    ]
    for _, axis, peer in sorted(order, key=lambda item: -item[0]):
        pl.semaphore_signal(
            sem, inc=1, device_id={axis: peer}, device_id_type=pl.DeviceIdType.MESH
        )


def wait_all(others):
    pl.semaphore_wait(pltpu.get_barrier_semaphore(), sum(map(len, others.values())))


def step_kernel(
    grp,
    region,
    pos,
    trans_hbm,
    meas_hbm,
    probe_hbm,
    k_hbm,
    steps_hbm,
    changes_hbm,
    old_hbm,
    data_ref,
    direction_ref,
    trans,
    meas,
    probe,
    kmat,
    steps,
    changes,
    old,
    x_send,
    x_recv,
    f_send,
    f_recv,
    b_send,
    b_recv,
    g_send,
    g_recv,
    one_send,
    one_recv,
    two_recv,
    select,
    put,
    wave,
    target,
    back_r,
    back_i,
    tile,
    gram,
    gradient,
    change,
    load_sem,
    send_sem,
    recv_sem,
    two_send_sem,
    two_recv_sem,
):
    me, here = lax.axis_index("grp"), lax.axis_index("region")
    cols, length = trans.shape[1], trans.shape[2]
    modes, rows, n = probe.shape[1], probe.shape[2], probe.shape[3]
    tiles = n // LANES
    parts = 2
    width = n // (grp * parts)
    per_part = tiles // parts
    part = n // parts
    depth = steps.shape[0]
    last = depth - 1
    groups = LANES // width
    slots = (groups // 2 - 1, groups - 1)
    loads = [
        pltpu.make_async_copy(src, dst, load_sem.at[i])
        for i, (src, dst) in enumerate(
            (
                (trans_hbm, trans),
                (meas_hbm, meas),
                (probe_hbm, probe),
                (k_hbm, kmat),
                (steps_hbm, steps),
                (changes_hbm, changes),
                (old_hbm, old),
            )
        )
    ]
    for load in loads[:2]:
        load.start()
    others = {axis: peers(axis) for axis in ("grp", "region")}
    signal_all(others)
    row0, col0 = pos[0, 0], pos[0, 1]
    phase = [0]
    copies = []

    def exchange(src, dst):
        at = phase[0]
        phase[0] += 1
        copies.append(Exchange("grp", others["grp"], src, dst, send_sem.at[at], recv_sem.at[at]))
        return copies[-1]

    pick = iota((n, length), 1) == iota((n, length), 0) + row0
    put[...] = pick.astype(F32).astype(BF16)
    group = iota((rows, LANES), 1) // width
    for load in loads[:2]:
        load.wait()
    for load in loads[2:]:
        load.start()
    gap = jnp.zeros((LANES // 2 - cols, length), F32)
    block = jnp.concatenate([trans[0], gap, trans[1], gap], axis=0).astype(BF16)
    seen = dot_t(put[...], block)
    for d in range(grp):
        value = seen[rows * d : rows * (d + 1)]
        for h, at in enumerate(slots):
            t, g = per_part * h + d // groups, d % groups
            moved = pltpu.roll(meas[0, :, LANES * t : LANES * (t + 1)], (width * (at - g)) % LANES, 1)
            value = jnp.where(group == at, moved, value)
        x_send[d] = value.astype(BF16)
    x_recv[me] = x_send[me]

    wait_all(others)
    x_copy = exchange(lambda p: x_send.at[p], lambda s: x_recv.at[s])
    x_copy.start()

    for d in range(grp):
        lane = iota((n, LANES), 1) % (LANES // 2)
        hit = (lane + cols * d == iota((n, LANES), 0) + col0) & (lane < cols)
        select[:, LANES * d : LANES * (d + 1)] = hit.astype(F32).astype(BF16)
    loads[2].wait()
    loads[3].wait()
    x_copy.wait_recv()
    first = iota((rows, LANES), 1) < LANES // 2
    stacked = []
    for d in range(grp):
        x = x_recv[d].astype(F32)
        zero = jnp.zeros_like(x)
        stacked.append(
            jnp.concatenate([jnp.where(first, x, zero), jnp.where(first, zero, x), zero, zero], axis=0).astype(BF16)
        )
    window = jnp.transpose(dot_t(select[...], jnp.concatenate(stacked, axis=1)))
    win_r, win_i = window[:rows], window[rows : 2 * rows]
    for m in range(modes):
        p_r, p_i = probe[0, m].astype(F32), probe[1, m].astype(F32)
        wave[0, rows * m : rows * (m + 1)] = (p_r * win_r - p_i * win_i).astype(BF16)
        wave[1, rows * m : rows * (m + 1)] = (p_r * win_i + p_i * win_r).astype(BF16)

    f_copies, b_copies = [], []
    for q in range(parts):
        span = slice(part * q, part * (q + 1))
        k_r, k_i = kmat[0, :, span], kmat[1, :, span]
        out = (
            dot(wave[0], k_r) - dot(wave[1], k_i),
            dot(wave[0], k_i) + dot(wave[1], k_r),
        )
        for c in range(2):
            for t in range(per_part):
                packed = swap(
                    [out[c][rows * m : rows * (m + 1), LANES * t : LANES * (t + 1)] for m in range(modes)]
                )
                for g in range(8):
                    f_send[q, 8 * t + g, :, LANES * c : LANES * (c + 1)] = packed[g].astype(BF16)
        f_recv[q, me] = f_send[q, me]
        f_copies.append(exchange(lambda p, q=q: f_send.at[q, p], lambda s, q=q: f_recv.at[q, s]))
        f_copies[q].start()

    seen = x_recv[...].astype(F32).reshape(n, LANES)
    group = iota((n, LANES), 1) // width
    for h, at in enumerate(slots):
        target[h] = spread_sum(jnp.where(group == at, seen, jnp.zeros_like(seen)), width)

    for load in loads[4:]:
        load.wait()
    spots = [
        (c, slice(8 * j, 8 * j + 8), slice(LANES * t, LANES * (t + 1)))
        for c in range(2)
        for j in range(cols // 8)
        for t in range(length // LANES)
    ]
    early, late = [], []
    for i in range(depth):
        early.append(("ss", i, i))
        late += [("sg", i, i), ("yg", i, i), ("sy", i, last), ("yy", i, last)]
        for j in range(i, last):
            early += [("sy", i, j), ("yy", i, j)]
    number = {name: at for at, name in enumerate(early + late)}

    def accumulate(names, vectors):
        sums = [None] * len(names)
        for at in spots:
            value = vectors(at)
            for e, (kind, a, b) in enumerate(names):
                left = value[kind[0]][a]
                right = value["g"] if kind[1] == "g" else value[kind[1]][b]
                sums[e] = left * right if sums[e] is None else sums[e] + left * right
        for name, total in zip(names, sums):
            gram[number[name] : number[name] + 1, :] = jnp.sum(total, axis=0, keepdims=True)

    def known(at):
        return {
            "s": [steps[(i, *at)] for i in range(depth)],
            "y": [changes[(i, *at)] for i in range(last)],
        }

    accumulate(early, known)

    for q in range(parts):
        f_copies[q].wait_recv()
        x = f_recv[q].reshape(n, 2 * LANES)
        by_r, by_i = dot(kmat[0], x), dot(kmat[1], x)
        d_r = (by_r[:, :LANES] - by_i[:, LANES:]).astype(BF16).astype(F32)
        d_i = (by_r[:, LANES:] + by_i[:, :LANES]).astype(BF16).astype(F32)
        misfit = spread_sum(d_r * d_r + d_i * d_i, width) - target[q]
        e = jnp.concatenate([(misfit * d_r).astype(BF16), (misfit * d_i).astype(BF16)], axis=1)
        by_r, by_i = dot(kmat[0], e), dot(kmat[1], e)
        b_send[q, :, :, :LANES] = (by_r[:, :LANES] + by_i[:, LANES:]).astype(BF16).reshape(grp, rows, LANES)
        b_send[q, :, :, LANES:] = (by_r[:, LANES:] - by_i[:, :LANES]).astype(BF16).reshape(grp, rows, LANES)
        b_recv[q, me] = b_send[q, me]
        b_copies.append(exchange(lambda p, q=q: b_send.at[q, p], lambda s, q=q: b_recv.at[q, s]))
        b_copies[q].start()

    for q in range(parts):
        b_copies[q].wait_recv()
        back = []
        for c in range(2):
            by_tile = []
            for t in range(per_part):
                packed = swap(
                    [b_recv[q, 8 * t + g, :, LANES * c : LANES * (c + 1)].astype(F32) for g in range(8)]
                )
                by_tile.append(jnp.concatenate(packed, axis=0))
            back.append(jnp.concatenate(by_tile, axis=1).astype(BF16))
        span = slice(part * q, part * (q + 1))
        k_r, k_i = kmat[0, span, :], kmat[1, span, :]
        p_r = dot(back[0], k_r) + dot(back[1], k_i)
        p_i = dot(back[1], k_r) - dot(back[0], k_i)
        if q == 0:
            back_r[...] = p_r
            back_i[...] = p_i
        else:
            back_r[...] += p_r
            back_i[...] += p_i
    grad_r = jnp.zeros((rows, n), F32)
    grad_i = jnp.zeros((rows, n), F32)
    for m in range(modes):
        w_r, w_i = probe[0, m].astype(F32), probe[1, m].astype(F32)
        o_r, o_i = back_r[rows * m : rows * (m + 1)], back_i[rows * m : rows * (m + 1)]
        grad_r = grad_r + (w_r * o_r + w_i * o_i)
        grad_i = grad_i + (w_r * o_i - w_i * o_r)

    grad_r = (4.0 * grad_r).astype(BF16)
    grad_i = (4.0 * grad_i).astype(BF16)
    place = iota((length, n), 0) == iota((length, n), 1) + col0
    tall = dot_t(
        place.astype(F32).astype(BF16), jnp.concatenate([grad_r] * 4 + [grad_i] * 4, axis=0)
    )
    tall = tall.reshape(grp, cols // 8, 8, 2 * LANES)
    pieces = [
        tall[:, j, :, LANES * c : LANES * (c + 1)] for c in range(2) for j in range(cols // 8)
    ]
    group = iota((grp, 8, LANES), 2) // 32
    zero = jnp.zeros((grp, 8, LANES), F32)
    wide = []
    for w in range(4):
        value = zero
        for p in range(4):
            if 4 * w + p < len(pieces):
                value = jnp.where(group == p, pieces[4 * w + p], value)
        wide.append(value)
    g_send[...] = jnp.concatenate(wide, axis=1).astype(BF16)
    g_recv[me] = g_send[me]
    g_copy = exchange(lambda p: g_send.at[p], lambda s: g_recv.at[s])
    g_copy.start()
    g_copy.wait_recv()
    for t in range(tiles):
        whole = [g_recv[4 * t + g].astype(F32) for g in range(4)]
        for w in range((len(pieces) + 3) // 4):
            packed = swap([x[8 * w : 8 * w + 8] for x in whole])
            for p in range(4):
                if 4 * w + p < len(pieces):
                    at = 8 * (4 * w + p)
                    tile[at : at + 8, LANES * t : LANES * (t + 1)] = packed[p]
    out = dot(tile[...].astype(BF16), put[...])
    data_ref[0] = out[:cols]
    data_ref[1] = out[cols:]

    def fresh(at):
        grad = data_ref[at] + TIKHONOV * trans[at]
        new = grad - old[at]
        gradient[at] = grad
        change[at] = new
        value = known(at)
        value["y"].append(new)
        value["g"] = grad
        return value

    accumulate(late, fresh)
    totals = jnp.sum(gram[...], axis=1, keepdims=True)
    count = gram.shape[0]
    totals = jnp.where(
        iota((count, LANES), 0) == iota((count, LANES), 1), totals, jnp.zeros((count, LANES), F32)
    )
    value = jnp.sum(totals, axis=0, keepdims=True)
    one_send[0] = value
    one_recv[me] = value
    one = exchange(lambda p: one_send.at[0], lambda s: one_recv.at[s])
    one.start()
    one.wait_recv()
    value = jnp.sum(one_recv[...], axis=0)
    one_send[1] = value
    two_recv[here] = value
    two = Exchange(
        "region",
        others["region"],
        lambda p: one_send.at[1],
        lambda s: two_recv.at[s],
        two_send_sem,
        two_recv_sem,
    )
    two.start()
    two.wait_recv()
    value = jnp.sum(two_recv[...], axis=0)

    def inner(kind, a, b):
        at = number[(kind, a, b)]
        return value[:, at : at + 1]

    curve = [
        jnp.maximum(inner("sy", i, i), CURVE_FLOOR * inner("ss", i, i)) for i in range(depth)
    ]
    alphas = [None] * depth
    for i in reversed(range(depth)):
        along = inner("sg", i, i)
        for j in range(i + 1, depth):
            along = along - alphas[j] * inner("sy", i, j)
        alphas[i] = along / curve[i]
    scale = curve[last] / (inner("yy", last, last) + EPSILON)
    weights = []
    for i in range(depth):
        along = inner("yg", i, i)
        for j in range(depth):
            along = along - alphas[j] * inner("yy", min(i, j), max(i, j))
        along = scale * along
        for j in range(i):
            along = along + weights[j] * inner("sy", j, i)
        weights.append(alphas[i] - along / curve[i])
    wide = lambda x: jnp.broadcast_to(x, (8, LANES))
    alphas = [wide(scale * alpha) for alpha in alphas]
    weights = [wide(weight) for weight in weights]
    scale = wide(scale)
    for at in spots:
        direction = scale * gradient[at]
        for i in range(depth):
            y = change[at] if i == last else changes[(i, *at)]
            direction = direction - alphas[i] * y + weights[i] * steps[(i, *at)]
        direction_ref[at] = direction
    for copy in (*copies, two):
        copy.wait_send()


def shards(grp, region, transmission, probe, measured, positions, past_steps, past_changes, old_gradient):
    two, cols, length = transmission.shape
    _, modes, rows, n = probe.shape
    parts = 2
    phases = 3 + 2 * parts
    vmem = pl.BlockSpec(memory_space=pltpu.VMEM)
    hbm = pl.BlockSpec(memory_space=pltpu.HBM)
    shape = jax.ShapeDtypeStruct((two, cols, length), F32)
    block = (parts, grp, rows, 2 * LANES)
    data, direction = pl.pallas_call(
        functools.partial(step_kernel, grp, region),
        out_shape=(shape, shape),
        in_specs=[pl.BlockSpec(memory_space=pltpu.SMEM)] + [hbm] * 7,
        out_specs=(vmem, vmem),
        scratch_shapes=[
            pltpu.VMEM((two, cols, length), F32),
            pltpu.VMEM(measured.shape, F32),
            pltpu.VMEM(probe.shape, BF16),
            pltpu.VMEM((2, n, n), BF16),
            pltpu.VMEM(past_steps.shape, F32),
            pltpu.VMEM(past_changes.shape, F32),
            pltpu.VMEM((two, cols, length), F32),
            pltpu.VMEM((grp, rows, LANES), BF16),
            pltpu.VMEM((grp, rows, LANES), BF16),
            pltpu.VMEM(block, BF16),
            pltpu.VMEM(block, BF16),
            pltpu.VMEM(block, BF16),
            pltpu.VMEM(block, BF16),
            pltpu.VMEM((grp, 32, LANES), BF16),
            pltpu.VMEM((grp, 32, LANES), BF16),
            pltpu.VMEM((2, 1, LANES), F32),
            pltpu.VMEM((grp, 1, LANES), F32),
            pltpu.VMEM((region, 1, LANES), F32),
            pltpu.VMEM((n, grp * LANES), BF16),
            pltpu.VMEM((n, length), BF16),
            pltpu.VMEM((2, modes * rows, n), BF16),
            pltpu.VMEM((parts, n, LANES), F32),
            pltpu.VMEM((modes * rows, n), F32),
            pltpu.VMEM((modes * rows, n), F32),
            pltpu.VMEM((two * cols, n), F32),
            pltpu.VMEM((32, LANES), F32),
            pltpu.VMEM((two, cols, length), F32),
            pltpu.VMEM((two, cols, length), F32),
            pltpu.SemaphoreType.DMA((7,)),
            pltpu.SemaphoreType.DMA((phases, grp)),
            pltpu.SemaphoreType.DMA((phases, grp)),
            pltpu.SemaphoreType.DMA((region,)),
            pltpu.SemaphoreType.DMA((region,)),
        ],
        compiler_params=pltpu.CompilerParams(
            collective_id=0, has_side_effects=True, vmem_limit_bytes=58 << 20
        ),
        name="step",
    )(
        positions,
        transmission,
        measured,
        probe,
        jnp.asarray(propagator(n)),
        past_steps,
        past_changes,
        old_gradient,
    )
    return transmission - direction, data + TIKHONOV * transmission


def solution(mesh):
    return jax.shard_map(
        functools.partial(shards, mesh.shape["grp"], mesh.shape["region"]),
        mesh=mesh,
        in_specs=(
            P(None, "grp", "region"),
            P(None, None, "grp", None),
            P("region", "grp", None),
            P("region", None),
            P(None, None, "grp", "region"),
            P(None, None, "grp", "region"),
            P(None, "grp", "region"),
        ),
        out_specs=(P(None, "grp", "region"), P(None, "grp", "region")),
        check_vma=False,
    )
```

```python
import functools
import itertools

import jax
import jax.numpy as jnp
import ml_dtypes
import numpy as np
from jax import lax
from jax.experimental import pallas as pl
from jax.experimental.pallas import tpu as pltpu
from jax.sharding import PartitionSpec as P

CURVE_FLOOR = 0.25
TIKHONOV = 0.5
EPSILON = 1e-06
F32 = jnp.float32
BF16 = jnp.bfloat16
LANES = 128


def propagator(count):
    index = np.arange(count)
    phase = np.outer(index, index) % count * (2.0 * np.pi / count)
    factor = 1.0 / np.sqrt(count)
    real = (np.cos(phase) * factor).astype(np.float32).astype(ml_dtypes.bfloat16)
    imag = (-np.sin(phase) * factor).astype(np.float32).astype(ml_dtypes.bfloat16)
    table = real.astype(np.float64) + 1j * imag.astype(np.float64)
    wavenumber = (index + count // 2) % count - count // 2
    chirp = np.exp(-2j * np.pi * (wavenumber * wavenumber % (4 * count)) / (4 * count))
    folded = (table * chirp[None, :]) @ table.conj()
    return np.stack([folded.real, folded.imag]).astype(np.float32).astype(ml_dtypes.bfloat16)


def dot(left, right):
    return jnp.dot(left, right, preferred_element_type=F32)


def dot_t(left, right):
    return lax.dot_general(left, right, (((1,), (1,)), ((), ())), preferred_element_type=F32)


def iota(shape, dim):
    return lax.broadcasted_iota(jnp.int32, shape, dim)


def swap(parts):
    count = len(parts)
    width = LANES // count
    lane = iota(parts[0].shape, 1)
    step = count // 2
    while step:
        low = lane % (2 * step * width) < step * width
        out = list(parts)
        for i in range(count):
            if i & step == 0:
                a, b = parts[i], parts[i + step]
                out[i] = jnp.where(low, a, pltpu.roll(b, step * width, 1))
                out[i + step] = jnp.where(low, pltpu.roll(a, LANES - step * width, 1), b)
        parts = out
        step //= 2
    return parts


def spread_sum(x, width):
    step = LANES // 2
    while step >= width:
        x = x + pltpu.roll(x, step, 1)
        step //= 2
    return x


LAYOUT = {"grp": ((8, 1), (2, 2)), "region": ((8, 1), (2, 1), (2, 0.25))}


def hops(axis, offset):
    return sum(min(o, size - o) * far for o, (size, far) in zip(offset, LAYOUT[axis]))


ORDER = {
    axis: sorted(
        (offset for offset in itertools.product(*(range(size) for size, _ in layout)) if any(offset)),
        key=lambda offset, axis=axis: -hops(axis, offset),
    )
    for axis, layout in LAYOUT.items()
}


def peers(axis):
    me = lax.axis_index(axis)
    digits, unit = [], 1
    for size, _ in reversed(LAYOUT[axis]):
        digits.insert(0, lax.rem(lax.div(me, unit), size))
        unit *= size
    found = []
    for offset in ORDER[axis]:
        peer = 0
        for o, digit, (size, _) in zip(offset, digits, LAYOUT[axis]):
            peer = peer * size + (lax.rem(digit + o, size) if o else digit)
        found.append(peer)
    return found


class Exchange:
    def __init__(self, axis, others, src, dst, send, recv):
        self.axis, self.others, self.src, self.dst, self.send, self.recv = axis, others, src, dst, send, recv
        self.me = lax.axis_index(axis)

    def copy(self, peer, slot):
        return pltpu.make_async_remote_copy(
            src_ref=self.src(peer),
            dst_ref=self.dst(slot),
            send_sem=self.send.at[peer],
            recv_sem=self.recv.at[slot],
            device_id={self.axis: peer},
            device_id_type=pl.DeviceIdType.MESH,
        )

    def each(self, act):
        for peer in self.others:
            act(peer)

    def start(self):
        self.each(lambda peer: self.copy(peer, self.me).start())

    def wait_recv(self):
        self.each(lambda peer: self.copy(peer, peer).wait_recv())

    def wait_send(self):
        self.each(lambda peer: self.copy(peer, self.me).wait_send())


def signal_all(others):
    sem = pltpu.get_barrier_semaphore()
    order = [
        (hops(axis, offset), axis, peer)
        for axis, members in others.items()
        for offset, peer in zip(ORDER[axis], members)
    ]
    for _, axis, peer in sorted(order, key=lambda item: -item[0]):
        pl.semaphore_signal(
            sem, inc=1, device_id={axis: peer}, device_id_type=pl.DeviceIdType.MESH
        )


def wait_all(others):
    pl.semaphore_wait(pltpu.get_barrier_semaphore(), sum(map(len, others.values())))


def step_kernel(
    grp,
    region,
    pos_hbm,
    trans_hbm,
    meas_hbm,
    probe_hbm,
    k_hbm,
    steps_hbm,
    changes_hbm,
    old_hbm,
    data_ref,
    direction_ref,
    pos,
    trans,
    meas,
    probe,
    kmat,
    steps,
    changes,
    old,
    x_send,
    x_recv,
    f_send,
    f_recv,
    b_send,
    b_recv,
    g_send,
    g_recv,
    one_send,
    one_recv,
    two_recv,
    select,
    put,
    wave,
    target,
    back_r,
    back_i,
    tile,
    gram,
    gradient,
    change,
    load_sem,
    send_sem,
    recv_sem,
    two_send_sem,
    two_recv_sem,
):
    me, here = lax.axis_index("grp"), lax.axis_index("region")
    cols, length = trans.shape[1], trans.shape[2]
    modes, rows, n = probe.shape[1], probe.shape[2], probe.shape[3]
    tiles = n // LANES
    parts = 2
    width = n // (grp * parts)
    per_part = tiles // parts
    part = n // parts
    depth = steps.shape[0]
    last = depth - 1
    groups = LANES // width
    slots = (groups // 2 - 1, groups - 1)
    loads = [
        pltpu.make_async_copy(src, dst, load_sem.at[i])
        for i, (src, dst) in enumerate(
            (
                (pos_hbm, pos),
                (trans_hbm, trans),
                (meas_hbm, meas),
                (probe_hbm, probe),
                (k_hbm, kmat),
                (steps_hbm, steps),
                (changes_hbm, changes),
                (old_hbm, old),
            )
        )
    ]
    for load in loads[:3]:
        load.start()
    others = {axis: peers(axis) for axis in ("grp", "region")}
    signal_all(others)
    loads[0].wait()
    row0, col0 = pos[0, 0], pos[0, 1]
    phase = [0]
    copies = []

    def exchange(src, dst):
        at = phase[0]
        phase[0] += 1
        copies.append(Exchange("grp", others["grp"], src, dst, send_sem.at[at], recv_sem.at[at]))
        return copies[-1]

    pick = iota((n, length), 1) == iota((n, length), 0) + row0
    put[...] = pick.astype(F32).astype(BF16)
    group = iota((rows, LANES), 1) // width
    for load in loads[1:3]:
        load.wait()
    for load in loads[3:]:
        load.start()
    gap = jnp.zeros((LANES // 2 - cols, length), F32)
    block = jnp.concatenate([trans[0], gap, trans[1], gap], axis=0).astype(BF16)
    seen = dot_t(put[...], block)
    for d in range(grp):
        value = seen[rows * d : rows * (d + 1)]
        for h, at in enumerate(slots):
            t, g = per_part * h + d // groups, d % groups
            moved = pltpu.roll(meas[0, :, LANES * t : LANES * (t + 1)], (width * (at - g)) % LANES, 1)
            value = jnp.where(group == at, moved, value)
        x_send[d] = value.astype(BF16)
    x_recv[me] = x_send[me]

    wait_all(others)
    x_copy = exchange(lambda p: x_send.at[p], lambda s: x_recv.at[s])
    x_copy.start()

    for d in range(grp):
        lane = iota((n, LANES), 1) % (LANES // 2)
        hit = (lane + cols * d == iota((n, LANES), 0) + col0) & (lane < cols)
        select[:, LANES * d : LANES * (d + 1)] = hit.astype(F32).astype(BF16)
    loads[3].wait()
    loads[4].wait()
    x_copy.wait_recv()
    first = iota((rows, LANES), 1) < LANES // 2
    stacked = []
    for d in range(grp):
        x = x_recv[d].astype(F32)
        zero = jnp.zeros_like(x)
        stacked.append(
            jnp.concatenate([jnp.where(first, x, zero), jnp.where(first, zero, x), zero, zero], axis=0).astype(BF16)
        )
    window = jnp.transpose(dot_t(select[...], jnp.concatenate(stacked, axis=1)))
    win_r, win_i = window[:rows], window[rows : 2 * rows]
    for m in range(modes):
        p_r, p_i = probe[0, m].astype(F32), probe[1, m].astype(F32)
        wave[0, rows * m : rows * (m + 1)] = (p_r * win_r - p_i * win_i).astype(BF16)
        wave[1, rows * m : rows * (m + 1)] = (p_r * win_i + p_i * win_r).astype(BF16)

    f_copies, b_copies = [], []
    for q in range(parts):
        span = slice(part * q, part * (q + 1))
        k_r, k_i = kmat[0, :, span], kmat[1, :, span]
        out = (
            dot(wave[0], k_r) - dot(wave[1], k_i),
            dot(wave[0], k_i) + dot(wave[1], k_r),
        )
        for c in range(2):
            for t in range(per_part):
                packed = swap(
                    [out[c][rows * m : rows * (m + 1), LANES * t : LANES * (t + 1)] for m in range(modes)]
                )
                for g in range(8):
                    f_send[q, 8 * t + g, :, LANES * c : LANES * (c + 1)] = packed[g].astype(BF16)
        f_recv[q, me] = f_send[q, me]
        f_copies.append(exchange(lambda p, q=q: f_send.at[q, p], lambda s, q=q: f_recv.at[q, s]))
        f_copies[q].start()

    seen = x_recv[...].astype(F32).reshape(n, LANES)
    group = iota((n, LANES), 1) // width
    for h, at in enumerate(slots):
        target[h] = spread_sum(jnp.where(group == at, seen, jnp.zeros_like(seen)), width)

    for load in loads[5:]:
        load.wait()
    spots = [
        (c, slice(8 * j, 8 * j + 8), slice(LANES * t, LANES * (t + 1)))
        for c in range(2)
        for j in range(cols // 8)
        for t in range(length // LANES)
    ]
    early, late = [], []
    for i in range(depth):
        early.append(("ss", i, i))
        late += [("sg", i, i), ("yg", i, i), ("sy", i, last), ("yy", i, last)]
        for j in range(i, last):
            early += [("sy", i, j), ("yy", i, j)]
    number = {name: at for at, name in enumerate(early + late)}

    def accumulate(names, vectors):
        sums = [None] * len(names)
        for at in spots:
            value = vectors(at)
            for e, (kind, a, b) in enumerate(names):
                left = value[kind[0]][a]
                right = value["g"] if kind[1] == "g" else value[kind[1]][b]
                sums[e] = left * right if sums[e] is None else sums[e] + left * right
        for name, total in zip(names, sums):
            gram[number[name] : number[name] + 1, :] = jnp.sum(total, axis=0, keepdims=True)

    def known(at):
        return {
            "s": [steps[(i, *at)] for i in range(depth)],
            "y": [changes[(i, *at)] for i in range(last)],
        }

    accumulate(early, known)

    for q in range(parts):
        f_copies[q].wait_recv()
        x = f_recv[q].reshape(n, 2 * LANES)
        by_r, by_i = dot(kmat[0], x), dot(kmat[1], x)
        d_r = (by_r[:, :LANES] - by_i[:, LANES:]).astype(BF16).astype(F32)
        d_i = (by_r[:, LANES:] + by_i[:, :LANES]).astype(BF16).astype(F32)
        misfit = spread_sum(d_r * d_r + d_i * d_i, width) - target[q]
        e = jnp.concatenate([(misfit * d_r).astype(BF16), (misfit * d_i).astype(BF16)], axis=1)
        by_r, by_i = dot(kmat[0], e), dot(kmat[1], e)
        b_send[q, :, :, :LANES] = (by_r[:, :LANES] + by_i[:, LANES:]).astype(BF16).reshape(grp, rows, LANES)
        b_send[q, :, :, LANES:] = (by_r[:, LANES:] - by_i[:, :LANES]).astype(BF16).reshape(grp, rows, LANES)
        b_recv[q, me] = b_send[q, me]
        b_copies.append(exchange(lambda p, q=q: b_send.at[q, p], lambda s, q=q: b_recv.at[q, s]))
        b_copies[q].start()

    for q in range(parts):
        b_copies[q].wait_recv()
        back = []
        for c in range(2):
            by_tile = []
            for t in range(per_part):
                packed = swap(
                    [b_recv[q, 8 * t + g, :, LANES * c : LANES * (c + 1)].astype(F32) for g in range(8)]
                )
                by_tile.append(jnp.concatenate(packed, axis=0))
            back.append(jnp.concatenate(by_tile, axis=1).astype(BF16))
        span = slice(part * q, part * (q + 1))
        k_r, k_i = kmat[0, span, :], kmat[1, span, :]
        p_r = dot(back[0], k_r) + dot(back[1], k_i)
        p_i = dot(back[1], k_r) - dot(back[0], k_i)
        if q == 0:
            back_r[...] = p_r
            back_i[...] = p_i
        else:
            back_r[...] += p_r
            back_i[...] += p_i
    grad_r = jnp.zeros((rows, n), F32)
    grad_i = jnp.zeros((rows, n), F32)
    for m in range(modes):
        w_r, w_i = probe[0, m].astype(F32), probe[1, m].astype(F32)
        o_r, o_i = back_r[rows * m : rows * (m + 1)], back_i[rows * m : rows * (m + 1)]
        grad_r = grad_r + (w_r * o_r + w_i * o_i)
        grad_i = grad_i + (w_r * o_i - w_i * o_r)

    grad_r = (4.0 * grad_r).astype(BF16)
    grad_i = (4.0 * grad_i).astype(BF16)
    place = iota((length, n), 0) == iota((length, n), 1) + col0
    tall = dot_t(
        place.astype(F32).astype(BF16), jnp.concatenate([grad_r] * 4 + [grad_i] * 4, axis=0)
    )
    tall = tall.reshape(grp, cols // 8, 8, 2 * LANES)
    pieces = [
        tall[:, j, :, LANES * c : LANES * (c + 1)] for c in range(2) for j in range(cols // 8)
    ]
    group = iota((grp, 8, LANES), 2) // 32
    zero = jnp.zeros((grp, 8, LANES), F32)
    wide = []
    for w in range(4):
        value = zero
        for p in range(4):
            if 4 * w + p < len(pieces):
                value = jnp.where(group == p, pieces[4 * w + p], value)
        wide.append(value)
    g_send[...] = jnp.concatenate(wide, axis=1).astype(BF16)
    g_recv[me] = g_send[me]
    g_copy = exchange(lambda p: g_send.at[p], lambda s: g_recv.at[s])
    g_copy.start()
    g_copy.wait_recv()
    for t in range(tiles):
        whole = [g_recv[4 * t + g].astype(F32) for g in range(4)]
        for w in range((len(pieces) + 3) // 4):
            packed = swap([x[8 * w : 8 * w + 8] for x in whole])
            for p in range(4):
                if 4 * w + p < len(pieces):
                    at = 8 * (4 * w + p)
                    tile[at : at + 8, LANES * t : LANES * (t + 1)] = packed[p]
    out = dot(tile[...].astype(BF16), put[...])
    data_ref[0] = out[:cols]
    data_ref[1] = out[cols:]

    def fresh(at):
        grad = data_ref[at] + TIKHONOV * trans[at]
        new = grad - old[at]
        gradient[at] = grad
        change[at] = new
        value = known(at)
        value["y"].append(new)
        value["g"] = grad
        return value

    accumulate(late, fresh)
    totals = jnp.sum(gram[...], axis=1, keepdims=True)
    count = gram.shape[0]
    totals = jnp.where(
        iota((count, LANES), 0) == iota((count, LANES), 1), totals, jnp.zeros((count, LANES), F32)
    )
    value = jnp.sum(totals, axis=0, keepdims=True)
    one_send[0] = value
    one_recv[me] = value
    one = exchange(lambda p: one_send.at[0], lambda s: one_recv.at[s])
    one.start()
    one.wait_recv()
    value = jnp.sum(one_recv[...], axis=0)
    one_send[1] = value
    two_recv[here] = value
    two = Exchange(
        "region",
        others["region"],
        lambda p: one_send.at[1],
        lambda s: two_recv.at[s],
        two_send_sem,
        two_recv_sem,
    )
    two.start()
    two.wait_recv()
    value = jnp.sum(two_recv[...], axis=0)

    def inner(kind, a, b):
        at = number[(kind, a, b)]
        return value[:, at : at + 1]

    curve = [
        jnp.maximum(inner("sy", i, i), CURVE_FLOOR * inner("ss", i, i)) for i in range(depth)
    ]
    alphas = [None] * depth
    for i in reversed(range(depth)):
        along = inner("sg", i, i)
        for j in range(i + 1, depth):
            along = along - alphas[j] * inner("sy", i, j)
        alphas[i] = along / curve[i]
    scale = curve[last] / (inner("yy", last, last) + EPSILON)
    weights = []
    for i in range(depth):
        along = inner("yg", i, i)
        for j in range(depth):
            along = along - alphas[j] * inner("yy", min(i, j), max(i, j))
        along = scale * along
        for j in range(i):
            along = along + weights[j] * inner("sy", j, i)
        weights.append(alphas[i] - along / curve[i])
    wide = lambda x: jnp.broadcast_to(x, (8, LANES))
    alphas = [wide(scale * alpha) for alpha in alphas]
    weights = [wide(weight) for weight in weights]
    scale = wide(scale)
    for c in range(2):
        for at in spots:
            if at[0] != c:
                continue
            direction = scale * gradient[at]
            for i in range(depth):
                y = change[at] if i == last else changes[(i, *at)]
                direction = direction - alphas[i] * y + weights[i] * steps[(i, *at)]
            direction_ref[at] = direction
    for copy in (*copies, two):
        copy.wait_send()


def shards(grp, region, transmission, probe, measured, positions, past_steps, past_changes, old_gradient):
    two, cols, length = transmission.shape
    _, modes, rows, n = probe.shape
    parts = 2
    phases = 3 + 2 * parts
    hbm = pl.BlockSpec(memory_space=pltpu.HBM)
    shape = jax.ShapeDtypeStruct((two, cols, length), F32)
    block = (parts, grp, rows, 2 * LANES)
    data, direction = pl.pallas_call(
        functools.partial(step_kernel, grp, region),
        out_shape=(shape, shape),
        in_specs=[hbm] * 8,
        out_specs=(pl.BlockSpec(memory_space=pltpu.VMEM),) * 2,
        scratch_shapes=[
            pltpu.SMEM(positions.shape, jnp.int32),
            pltpu.VMEM((two, cols, length), F32),
            pltpu.VMEM(measured.shape, F32),
            pltpu.VMEM(probe.shape, BF16),
            pltpu.VMEM((2, n, n), BF16),
            pltpu.VMEM(past_steps.shape, F32),
            pltpu.VMEM(past_changes.shape, F32),
            pltpu.VMEM((two, cols, length), F32),
            pltpu.VMEM((grp, rows, LANES), BF16),
            pltpu.VMEM((grp, rows, LANES), BF16),
            pltpu.VMEM(block, BF16),
            pltpu.VMEM(block, BF16),
            pltpu.VMEM(block, BF16),
            pltpu.VMEM(block, BF16),
            pltpu.VMEM((grp, 32, LANES), BF16),
            pltpu.VMEM((grp, 32, LANES), BF16),
            pltpu.VMEM((2, 1, LANES), F32),
            pltpu.VMEM((grp, 1, LANES), F32),
            pltpu.VMEM((region, 1, LANES), F32),
            pltpu.VMEM((n, grp * LANES), BF16),
            pltpu.VMEM((n, length), BF16),
            pltpu.VMEM((2, modes * rows, n), BF16),
            pltpu.VMEM((parts, n, LANES), F32),
            pltpu.VMEM((modes * rows, n), F32),
            pltpu.VMEM((modes * rows, n), F32),
            pltpu.VMEM((two * cols, n), F32),
            pltpu.VMEM((32, LANES), F32),
            pltpu.VMEM((two, cols, length), F32),
            pltpu.VMEM((two, cols, length), F32),
            pltpu.SemaphoreType.DMA((8,)),
            pltpu.SemaphoreType.DMA((phases, grp)),
            pltpu.SemaphoreType.DMA((phases, grp)),
            pltpu.SemaphoreType.DMA((region,)),
            pltpu.SemaphoreType.DMA((region,)),
        ],
        compiler_params=pltpu.CompilerParams(
            collective_id=0, has_side_effects=True, vmem_limit_bytes=48 << 20
        ),
        name="step",
    )(
        *(
            pltpu.with_memory_space_constraint(operand, pltpu.HBM)
            for operand in (
                positions,
                transmission,
                measured,
                probe,
                jnp.asarray(propagator(n)),
                past_steps,
                past_changes,
                old_gradient,
            )
        )
    )
    return transmission - direction, data + TIKHONOV * transmission


def solution(mesh):
    return jax.shard_map(
        functools.partial(shards, mesh.shape["grp"], mesh.shape["region"]),
        mesh=mesh,
        in_specs=(
            P(None, "grp", "region"),
            P(None, None, "grp", None),
            P("region", "grp", None),
            P("region", None),
            P(None, None, "grp", "region"),
            P(None, None, "grp", "region"),
            P(None, "grp", "region"),
        ),
        out_specs=(P(None, "grp", "region"), P(None, "grp", "region")),
        check_vma=False,
    )
```

```python
import functools
import itertools

import jax
import jax.numpy as jnp
import ml_dtypes
import numpy as np
from jax import lax
from jax.experimental import pallas as pl
from jax.experimental.pallas import tpu as pltpu
from jax.sharding import PartitionSpec as P

CURVE_FLOOR = 0.25
TIKHONOV = 0.5
EPSILON = 1e-06
F32 = jnp.float32
BF16 = jnp.bfloat16
LANES = 128


def propagator(count):
    index = np.arange(count)
    phase = np.outer(index, index) % count * (2.0 * np.pi / count)
    factor = 1.0 / np.sqrt(count)
    real = (np.cos(phase) * factor).astype(np.float32).astype(ml_dtypes.bfloat16)
    imag = (-np.sin(phase) * factor).astype(np.float32).astype(ml_dtypes.bfloat16)
    table = real.astype(np.float64) + 1j * imag.astype(np.float64)
    wavenumber = (index + count // 2) % count - count // 2
    chirp = np.exp(-2j * np.pi * (wavenumber * wavenumber % (4 * count)) / (4 * count))
    folded = (table * chirp[None, :]) @ table.conj()
    return np.stack([folded.real, folded.imag]).astype(np.float32).astype(ml_dtypes.bfloat16)


def dot(left, right):
    return jnp.dot(left, right, preferred_element_type=F32)


def dot_t(left, right):
    return lax.dot_general(left, right, (((1,), (1,)), ((), ())), preferred_element_type=F32)


def iota(shape, dim):
    return lax.broadcasted_iota(jnp.int32, shape, dim)


def swap(parts):
    count = len(parts)
    width = LANES // count
    lane = iota(parts[0].shape, 1)
    step = count // 2
    while step:
        low = lane % (2 * step * width) < step * width
        out = list(parts)
        for i in range(count):
            if i & step == 0:
                a, b = parts[i], parts[i + step]
                out[i] = jnp.where(low, a, pltpu.roll(b, step * width, 1))
                out[i + step] = jnp.where(low, pltpu.roll(a, LANES - step * width, 1), b)
        parts = out
        step //= 2
    return parts


def spread_sum(x, width):
    step = LANES // 2
    while step >= width:
        x = x + pltpu.roll(x, step, 1)
        step //= 2
    return x


LAYOUT = {"grp": ((8, 1), (2, 2)), "region": ((8, 1), (2, 1), (2, 0.25))}


def hops(axis, offset):
    return sum(min(o, size - o) * far for o, (size, far) in zip(offset, LAYOUT[axis]))


ORDER = {
    axis: sorted(
        (offset for offset in itertools.product(*(range(size) for size, _ in layout)) if any(offset)),
        key=lambda offset, axis=axis: -hops(axis, offset),
    )
    for axis, layout in LAYOUT.items()
}


def peers(axis):
    me = lax.axis_index(axis)
    digits, unit = [], 1
    for size, _ in reversed(LAYOUT[axis]):
        digits.insert(0, lax.rem(lax.div(me, unit), size))
        unit *= size
    found = []
    for offset in ORDER[axis]:
        peer = 0
        for o, digit, (size, _) in zip(offset, digits, LAYOUT[axis]):
            peer = peer * size + (lax.rem(digit + o, size) if o else digit)
        found.append(peer)
    return found


class Exchange:
    def __init__(self, axis, others, src, dst, send, recv, shared=False):
        self.axis, self.others, self.src, self.dst = axis, others, src, dst
        self.send, self.recv, self.shared = send, recv, shared
        self.me = lax.axis_index(axis)

    def copy(self, src, dst):
        return pltpu.make_async_remote_copy(
            src_ref=src,
            dst_ref=dst,
            send_sem=self.send,
            recv_sem=self.recv,
            device_id={self.axis: self.others[0]},
            device_id_type=pl.DeviceIdType.MESH,
        )

    def start(self):
        for peer in self.others:
            pltpu.make_async_remote_copy(
                src_ref=self.src if self.shared else self.src.at[peer],
                dst_ref=self.dst.at[self.me],
                send_sem=self.send,
                recv_sem=self.recv,
                device_id={self.axis: peer},
                device_id_type=pl.DeviceIdType.MESH,
            ).start()

    def bulk(self):
        every = self.dst.at[pl.ds(0, len(self.others))]
        return self.copy(every, every)

    def wait_recv(self):
        self.bulk().wait_recv()

    def wait_send(self):
        self.bulk().wait_send()


def signal_all(others):
    sem = pltpu.get_barrier_semaphore()
    order = [
        (hops(axis, offset), axis, peer)
        for axis, members in others.items()
        for offset, peer in zip(ORDER[axis], members)
    ]
    for _, axis, peer in sorted(order, key=lambda item: -item[0]):
        pl.semaphore_signal(
            sem, inc=1, device_id={axis: peer}, device_id_type=pl.DeviceIdType.MESH
        )


def wait_all(others):
    pl.semaphore_wait(pltpu.get_barrier_semaphore(), sum(map(len, others.values())))


def step_kernel(
    grp,
    region,
    pos_hbm,
    trans_hbm,
    meas_hbm,
    probe_hbm,
    k_hbm,
    steps_hbm,
    changes_hbm,
    old_hbm,
    data_ref,
    direction_ref,
    pos,
    trans,
    meas,
    probe,
    kmat,
    steps,
    changes,
    old,
    x_send,
    x_recv,
    f_send,
    f_recv,
    b_send,
    b_recv,
    g_send,
    g_recv,
    one_send,
    one_recv,
    two_recv,
    select,
    put,
    wave,
    target,
    shift,
    tile,
    gram,
    gradient,
    change,
    load_sem,
    send_sem,
    recv_sem,
):
    me, here = lax.axis_index("grp"), lax.axis_index("region")
    cols, length = trans.shape[1], trans.shape[2]
    modes, rows, n = probe.shape[1], probe.shape[2], probe.shape[3]
    tiles = n // LANES
    parts = 2
    width = n // (grp * parts)
    per_part = tiles // parts
    part = n // parts
    depth = steps.shape[0]
    last = depth - 1
    groups = LANES // width
    slots = (groups // 2 - 1, groups - 1)
    loads = [
        pltpu.make_async_copy(src, dst, load_sem.at[i])
        for i, (src, dst) in enumerate(
            (
                (pos_hbm, pos),
                (trans_hbm, trans),
                (meas_hbm, meas),
                (probe_hbm, probe),
                (k_hbm, kmat),
                (steps_hbm, steps),
                (changes_hbm, changes),
                (old_hbm, old),
            )
        )
    ]
    for load in loads[:3]:
        load.start()
    others = {axis: peers(axis) for axis in ("grp", "region")}
    signal_all(others)
    loads[0].wait()
    row0, col0 = pos[0, 0], pos[0, 1]
    phase = [0]
    copies = []

    def exchange(src, dst, axis="grp", shared=False):
        at = phase[0]
        phase[0] += 1
        copies.append(Exchange(axis, others[axis], src, dst, send_sem.at[at], recv_sem.at[at], shared))
        return copies[-1]

    pick = iota((n, length), 1) == iota((n, length), 0) + row0
    put[...] = pick.astype(F32).astype(BF16)
    group = iota((rows, LANES), 1) // width
    for load in loads[1:3]:
        load.wait()
    for load in loads[3:]:
        load.start()
    gap = jnp.zeros((LANES // 2 - cols, length), F32)
    block = jnp.concatenate([trans[0], gap, trans[1], gap], axis=0).astype(BF16)
    seen = dot_t(put[...], block)
    for d in range(grp):
        value = seen[rows * d : rows * (d + 1)]
        for h, at in enumerate(slots):
            t, g = per_part * h + d // groups, d % groups
            moved = pltpu.roll(meas[0, :, LANES * t : LANES * (t + 1)], (width * (at - g)) % LANES, 1)
            value = jnp.where(group == at, moved, value)
        x_send[d] = value.astype(BF16)
    x_recv[me] = x_send[me]

    wait_all(others)
    x_copy = exchange(x_send, x_recv)
    x_copy.start()

    for d in range(grp):
        lane = iota((n, LANES), 1) % (LANES // 2)
        hit = (lane + cols * d == iota((n, LANES), 0) + col0) & (lane < cols)
        select[:, LANES * d : LANES * (d + 1)] = hit.astype(F32).astype(BF16)
    loads[3].wait()
    loads[4].wait()
    x_copy.wait_recv()
    first = iota((rows, LANES), 1) < LANES // 2
    stacked = []
    for d in range(grp):
        x = x_recv[d].astype(F32)
        zero = jnp.zeros_like(x)
        stacked.append(
            jnp.concatenate([jnp.where(first, x, zero), jnp.where(first, zero, x), zero, zero], axis=0).astype(BF16)
        )
    window = jnp.transpose(dot_t(select[...], jnp.concatenate(stacked, axis=1)))
    win_r, win_i = window[:rows], window[rows : 2 * rows]
    for m in range(modes):
        p_r, p_i = probe[0, m].astype(F32), probe[1, m].astype(F32)
        wave[0, rows * m : rows * (m + 1)] = (p_r * win_r - p_i * win_i).astype(BF16)
        wave[1, rows * m : rows * (m + 1)] = (p_r * win_i + p_i * win_r).astype(BF16)

    f_copies, b_copies = [], []
    for q in range(parts):
        span = slice(part * q, part * (q + 1))
        k_r, k_i = kmat[0, :, span], kmat[1, :, span]
        out = (
            dot(wave[0], k_r) - dot(wave[1], k_i),
            dot(wave[0], k_i) + dot(wave[1], k_r),
        )
        for c in range(2):
            for t in range(per_part):
                packed = swap(
                    [out[c][rows * m : rows * (m + 1), LANES * t : LANES * (t + 1)] for m in range(modes)]
                )
                for g in range(8):
                    f_send[q, 8 * t + g, :, LANES * c : LANES * (c + 1)] = packed[g].astype(BF16)
        f_recv[q, me] = f_send[q, me]
        f_copies.append(exchange(f_send.at[q], f_recv.at[q]))
        f_copies[q].start()

    seen = x_recv[...].astype(F32).reshape(n, LANES)
    group = iota((n, LANES), 1) // width
    for h, at in enumerate(slots):
        target[h] = spread_sum(jnp.where(group == at, seen, jnp.zeros_like(seen)), width)

    for load in loads[5:]:
        load.wait()
    spots = [
        (c, slice(8 * j, 8 * j + 8), slice(LANES * t, LANES * (t + 1)))
        for c in range(2)
        for j in range(cols // 8)
        for t in range(length // LANES)
    ]
    early, late = [], []
    for i in range(depth):
        early.append(("ss", i, i))
        late += [("sg", i, i), ("yg", i, i), ("sy", i, last), ("yy", i, last)]
        for j in range(i, last):
            early += [("sy", i, j), ("yy", i, j)]
    number = {name: at for at, name in enumerate(early + late)}

    def accumulate(names, vectors):
        sums = [None] * len(names)
        for at in spots:
            value = vectors(at)
            for e, (kind, a, b) in enumerate(names):
                left = value[kind[0]][a]
                right = value["g"] if kind[1] == "g" else value[kind[1]][b]
                sums[e] = left * right if sums[e] is None else sums[e] + left * right
        for name, total in zip(names, sums):
            gram[number[name] : number[name] + 1, :] = jnp.sum(total, axis=0, keepdims=True)

    def known(at):
        return {
            "s": [steps[(i, *at)] for i in range(depth)],
            "y": [changes[(i, *at)] for i in range(last)],
        }

    accumulate(early, known)

    for q in range(parts):
        f_copies[q].wait_recv()
        x = f_recv[q].reshape(n, 2 * LANES)
        by_r, by_i = dot(kmat[0], x), dot(kmat[1], x)
        d_r = (by_r[:, :LANES] - by_i[:, LANES:]).astype(BF16).astype(F32)
        d_i = (by_r[:, LANES:] + by_i[:, :LANES]).astype(BF16).astype(F32)
        misfit = spread_sum(d_r * d_r + d_i * d_i, width) - target[q]
        e = jnp.concatenate([(misfit * d_r).astype(BF16), (misfit * d_i).astype(BF16)], axis=1)
        by_r, by_i = dot(kmat[0], e), dot(kmat[1], e)
        b_send[q, :, :, :LANES] = (by_r[:, :LANES] + by_i[:, LANES:]).astype(BF16).reshape(grp, rows, LANES)
        b_send[q, :, :, LANES:] = (by_r[:, LANES:] - by_i[:, :LANES]).astype(BF16).reshape(grp, rows, LANES)
        b_recv[q, me] = b_send[q, me]
        b_copies.append(exchange(b_send.at[q], b_recv.at[q]))
        b_copies[q].start()

    place = iota((length, n), 0) == iota((length, n), 1) + col0
    shift[...] = place.astype(F32).astype(BF16)
    grad_r = jnp.zeros((rows, n), F32)
    grad_i = jnp.zeros((rows, n), F32)
    for q in range(parts):
        b_copies[q].wait_recv()
        back = []
        for c in range(2):
            by_tile = []
            for t in range(per_part):
                packed = swap(
                    [b_recv[q, 8 * t + g, :, LANES * c : LANES * (c + 1)].astype(F32) for g in range(8)]
                )
                by_tile.append(jnp.concatenate(packed, axis=0))
            back.append(jnp.concatenate(by_tile, axis=1).astype(BF16))
        span = slice(part * q, part * (q + 1))
        k_r, k_i = kmat[0, span, :], kmat[1, span, :]
        p_r = dot(back[0], k_r) + dot(back[1], k_i)
        p_i = dot(back[1], k_r) - dot(back[0], k_i)
        for m in range(modes):
            w_r, w_i = probe[0, m].astype(F32), probe[1, m].astype(F32)
            o_r, o_i = p_r[rows * m : rows * (m + 1)], p_i[rows * m : rows * (m + 1)]
            grad_r = grad_r + (w_r * o_r + w_i * o_i)
            grad_i = grad_i + (w_r * o_i - w_i * o_r)

    grad_r = (4.0 * grad_r).astype(BF16)
    grad_i = (4.0 * grad_i).astype(BF16)
    tall = dot_t(shift[...], jnp.concatenate([grad_r] * 4 + [grad_i] * 4, axis=0))
    tall = tall.reshape(grp, cols // 8, 8, 2 * LANES)
    pieces = [
        tall[:, j, :, LANES * c : LANES * (c + 1)] for c in range(2) for j in range(cols // 8)
    ]
    group = iota((grp, 8, LANES), 2) // 32
    zero = jnp.zeros((grp, 8, LANES), F32)
    wide = []
    for w in range(4):
        value = zero
        for p in range(4):
            if 4 * w + p < len(pieces):
                value = jnp.where(group == p, pieces[4 * w + p], value)
        wide.append(value)
    g_send[...] = jnp.concatenate(wide, axis=1).astype(BF16)
    g_recv[me] = g_send[me]
    g_copy = exchange(g_send, g_recv)
    g_copy.start()
    g_copy.wait_recv()
    for t in range(tiles):
        whole = [g_recv[4 * t + g].astype(F32) for g in range(4)]
        for w in range((len(pieces) + 3) // 4):
            packed = swap([x[8 * w : 8 * w + 8] for x in whole])
            for p in range(4):
                if 4 * w + p < len(pieces):
                    at = 8 * (4 * w + p)
                    tile[at : at + 8, LANES * t : LANES * (t + 1)] = packed[p]
    out = dot(tile[...].astype(BF16), put[...])
    data_ref[0] = out[:cols]
    data_ref[1] = out[cols:]

    def fresh(at):
        grad = data_ref[at] + TIKHONOV * trans[at]
        new = grad - old[at]
        gradient[at] = grad
        change[at] = new
        value = known(at)
        value["y"].append(new)
        value["g"] = grad
        return value

    accumulate(late, fresh)
    totals = jnp.sum(gram[...], axis=1, keepdims=True)
    count = gram.shape[0]
    totals = jnp.where(
        iota((count, LANES), 0) == iota((count, LANES), 1), totals, jnp.zeros((count, LANES), F32)
    )
    value = jnp.sum(totals, axis=0, keepdims=True)
    one_send[0] = value
    one_recv[me] = value
    one = exchange(one_send.at[0], one_recv, shared=True)
    one.start()
    one.wait_recv()
    value = jnp.sum(one_recv[...], axis=0)
    one_send[1] = value
    two_recv[here] = value
    two = exchange(one_send.at[1], two_recv, "region", shared=True)
    two.start()
    two.wait_recv()
    value = jnp.sum(two_recv[...], axis=0)

    def inner(kind, a, b):
        at = number[(kind, a, b)]
        return value[:, at : at + 1]

    curve = [
        jnp.maximum(inner("sy", i, i), CURVE_FLOOR * inner("ss", i, i)) for i in range(depth)
    ]
    alphas = [None] * depth
    for i in reversed(range(depth)):
        along = inner("sg", i, i)
        for j in range(i + 1, depth):
            along = along - alphas[j] * inner("sy", i, j)
        alphas[i] = along / curve[i]
    scale = curve[last] / (inner("yy", last, last) + EPSILON)
    weights = []
    for i in range(depth):
        along = inner("yg", i, i)
        for j in range(depth):
            along = along - alphas[j] * inner("yy", min(i, j), max(i, j))
        along = scale * along
        for j in range(i):
            along = along + weights[j] * inner("sy", j, i)
        weights.append(alphas[i] - along / curve[i])
    wide = lambda x: jnp.broadcast_to(x, (8, LANES))
    alphas = [wide(scale * alpha) for alpha in alphas]
    weights = [wide(weight) for weight in weights]
    scale = wide(scale)
    for c in range(2):
        for at in spots:
            if at[0] != c:
                continue
            direction = scale * gradient[at]
            for i in range(depth):
                y = change[at] if i == last else changes[(i, *at)]
                direction = direction - alphas[i] * y + weights[i] * steps[(i, *at)]
            direction_ref[at] = direction
    for copy in copies:
        copy.wait_send()


def shards(grp, region, transmission, probe, measured, positions, past_steps, past_changes, old_gradient):
    two, cols, length = transmission.shape
    _, modes, rows, n = probe.shape
    parts = 2
    phases = 4 + 2 * parts
    hbm = pl.BlockSpec(memory_space=pltpu.HBM)
    shape = jax.ShapeDtypeStruct((two, cols, length), F32)
    block = (parts, grp, rows, 2 * LANES)
    data, direction = pl.pallas_call(
        functools.partial(step_kernel, grp, region),
        out_shape=(shape, shape),
        in_specs=[hbm] * 8,
        out_specs=(pl.BlockSpec(memory_space=pltpu.VMEM),) * 2,
        scratch_shapes=[
            pltpu.SMEM(positions.shape, jnp.int32),
            pltpu.VMEM((two, cols, length), F32),
            pltpu.VMEM(measured.shape, F32),
            pltpu.VMEM(probe.shape, BF16),
            pltpu.VMEM((2, n, n), BF16),
            pltpu.VMEM(past_steps.shape, F32),
            pltpu.VMEM(past_changes.shape, F32),
            pltpu.VMEM((two, cols, length), F32),
            pltpu.VMEM((grp, rows, LANES), BF16),
            pltpu.VMEM((grp, rows, LANES), BF16),
            pltpu.VMEM(block, BF16),
            pltpu.VMEM(block, BF16),
            pltpu.VMEM(block, BF16),
            pltpu.VMEM(block, BF16),
            pltpu.VMEM((grp, 32, LANES), BF16),
            pltpu.VMEM((grp, 32, LANES), BF16),
            pltpu.VMEM((2, 1, LANES), F32),
            pltpu.VMEM((grp, 1, LANES), F32),
            pltpu.VMEM((region, 1, LANES), F32),
            pltpu.VMEM((n, grp * LANES), BF16),
            pltpu.VMEM((n, length), BF16),
            pltpu.VMEM((2, modes * rows, n), BF16),
            pltpu.VMEM((parts, n, LANES), F32),
            pltpu.VMEM((length, n), BF16),
            pltpu.VMEM((two * cols, n), F32),
            pltpu.VMEM((32, LANES), F32),
            pltpu.VMEM((two, cols, length), F32),
            pltpu.VMEM((two, cols, length), F32),
            pltpu.SemaphoreType.DMA((8,)),
            pltpu.SemaphoreType.DMA((phases,)),
            pltpu.SemaphoreType.DMA((phases,)),
        ],
        compiler_params=pltpu.CompilerParams(
            collective_id=0, has_side_effects=True, vmem_limit_bytes=48 << 20
        ),
        name="step",
    )(
        *(
            pltpu.with_memory_space_constraint(operand, pltpu.HBM)
            for operand in (
                positions,
                transmission,
                measured,
                probe,
                jnp.asarray(propagator(n)),
                past_steps,
                past_changes,
                old_gradient,
            )
        )
    )
    return transmission - direction, data + TIKHONOV * transmission


def solution(mesh):
    return jax.shard_map(
        functools.partial(shards, mesh.shape["grp"], mesh.shape["region"]),
        mesh=mesh,
        in_specs=(
            P(None, "grp", "region"),
            P(None, None, "grp", None),
            P("region", "grp", None),
            P("region", None),
            P(None, None, "grp", "region"),
            P(None, None, "grp", "region"),
            P(None, "grp", "region"),
        ),
        out_specs=(P(None, "grp", "region"), P(None, "grp", "region")),
        check_vma=False,
    )
```

```python
import functools
import itertools
import math

import jax
import jax.numpy as jnp
import ml_dtypes
import numpy as np
from jax import lax
from jax.experimental import pallas as pl
from jax.experimental.pallas import tpu as pltpu
from jax.sharding import PartitionSpec as P

CURVE_FLOOR = 0.25
TIKHONOV = 0.5
EPSILON = 1e-06
F32 = jnp.float32
BF16 = jnp.bfloat16
LANES = 128


def propagator(count):
    index = np.arange(count)
    phase = np.outer(index, index) % count * (2.0 * np.pi / count)
    factor = 1.0 / np.sqrt(count)
    real = (np.cos(phase) * factor).astype(np.float32).astype(ml_dtypes.bfloat16)
    imag = (-np.sin(phase) * factor).astype(np.float32).astype(ml_dtypes.bfloat16)
    table = real.astype(np.float64) + 1j * imag.astype(np.float64)
    wavenumber = (index + count // 2) % count - count // 2
    chirp = np.exp(-2j * np.pi * (wavenumber * wavenumber % (4 * count)) / (4 * count))
    folded = (table * chirp[None, :]) @ table.conj()
    return np.stack([folded.real, folded.imag]).astype(np.float32).astype(ml_dtypes.bfloat16)


def dot(left, right):
    return jnp.dot(left, right, preferred_element_type=F32)


def dot_t(left, right):
    return lax.dot_general(left, right, (((1,), (1,)), ((), ())), preferred_element_type=F32)


def iota(shape, dim):
    return lax.broadcasted_iota(jnp.int32, shape, dim)


def swap(parts):
    count = len(parts)
    width = LANES // count
    lane = iota(parts[0].shape, 1)
    step = count // 2
    while step:
        low = lane % (2 * step * width) < step * width
        out = list(parts)
        for i in range(count):
            if i & step == 0:
                a, b = parts[i], parts[i + step]
                out[i] = jnp.where(low, a, pltpu.roll(b, step * width, 1))
                out[i + step] = jnp.where(low, pltpu.roll(a, LANES - step * width, 1), b)
        parts = out
        step //= 2
    return parts


def spread_sum(x, width):
    step = LANES // 2
    while step >= width:
        x = x + pltpu.roll(x, step, 1)
        step //= 2
    return x


PLACE = {
    "z": ("grp", 2, 8),
    "x_hi": ("grp", 1, 2),
    "y": ("region", 4, 8),
    "x_lo": ("region", 2, 2),
    "core": ("region", 1, 2),
}
TEAMS = {"rows": ("z", "x_hi"), "plane": ("z", "x_hi", "x_lo"), "line": ("y", "core")}


def hops(step):
    z, y = (min(step.get(name, 0), 8 - step.get(name, 0)) for name in ("z", "y"))
    x = 2 * step.get("x_hi", 0) + step.get("x_lo", 0)
    return z + y + min(x, 4 - x) + 0.25 * step.get("core", 0)


class Team:
    def __init__(self, names, digits):
        self.size = math.prod(PLACE[name][2] for name in names)
        self.me = 0
        for name in names:
            self.me = self.me * PLACE[name][2] + digits[name]
        steps = itertools.product(*(range(PLACE[name][2]) for name in names))
        steps = [dict(zip(names, step)) for step in steps if any(step)]
        self.hops, self.others = [], []
        for step in sorted(steps, key=lambda step: -hops(step)):
            place, number = {}, 0
            for name in names:
                axis, unit, size = PLACE[name]
                digit = lax.rem(digits[name] + step[name], size) if step[name] else digits[name]
                number = number * size + digit
            for axis in sorted({PLACE[name][0] for name in names}):
                place[axis] = sum(
                    (lax.rem(digits[name] + step[name], size) if step.get(name) else digits[name]) * unit
                    for name, (on, unit, size) in PLACE.items()
                    if on == axis
                )
            self.hops.append(hops(step))
            self.others.append((number, place))


class Exchange:
    def __init__(self, team, src, dst, send, recv, shared=False):
        self.team, self.src, self.dst = team, src, dst
        self.send, self.recv, self.shared = send, recv, shared

    def copy(self, src, dst, place):
        return pltpu.make_async_remote_copy(
            src_ref=src,
            dst_ref=dst,
            send_sem=self.send,
            recv_sem=self.recv,
            device_id=place,
            device_id_type=pl.DeviceIdType.MESH,
        )

    def start(self):
        for number, place in self.team.others:
            src = self.src if self.shared else self.src.at[number]
            self.copy(src, self.dst.at[self.team.me], place).start()

    def bulk(self):
        every = self.dst.at[pl.ds(0, self.team.size - 1)]
        return self.copy(every, every, self.team.others[0][1])

    def wait_recv(self):
        self.bulk().wait_recv()

    def wait_send(self):
        self.bulk().wait_send()


def signal_all(teams):
    sem = pltpu.get_barrier_semaphore()
    order = [(far, place) for team in teams for far, (_, place) in zip(team.hops, team.others)]
    for _, place in sorted(order, key=lambda item: -item[0]):
        pl.semaphore_signal(sem, inc=1, device_id=place, device_id_type=pl.DeviceIdType.MESH)


def wait_all(teams):
    pl.semaphore_wait(pltpu.get_barrier_semaphore(), sum(team.size - 1 for team in teams))


def step_kernel(
    grp,
    region,
    pos_hbm,
    trans_hbm,
    meas_hbm,
    probe_hbm,
    k_hbm,
    steps_hbm,
    changes_hbm,
    old_hbm,
    data_ref,
    direction_ref,
    pos,
    trans,
    meas,
    probe,
    kmat,
    steps,
    changes,
    old,
    x_send,
    x_recv,
    f_send,
    f_recv,
    b_send,
    b_recv,
    g_send,
    g_recv,
    one_send,
    one_recv,
    two_recv,
    select,
    put,
    wave,
    target,
    shift,
    tile,
    gram,
    gradient,
    change,
    load_sem,
    send_sem,
    recv_sem,
):
    me = lax.axis_index("grp")
    cols, length = trans.shape[1], trans.shape[2]
    modes, rows, n = probe.shape[1], probe.shape[2], probe.shape[3]
    tiles = n // LANES
    parts = 2
    width = n // (grp * parts)
    per_part = tiles // parts
    part = n // parts
    depth = steps.shape[0]
    last = depth - 1
    groups = LANES // width
    slots = (groups // 2 - 1, groups - 1)
    loads = [
        pltpu.make_async_copy(src, dst, load_sem.at[i])
        for i, (src, dst) in enumerate(
            (
                (pos_hbm, pos),
                (trans_hbm, trans),
                (meas_hbm, meas),
                (probe_hbm, probe),
                (k_hbm, kmat),
                (steps_hbm, steps),
                (changes_hbm, changes),
                (old_hbm, old),
            )
        )
    ]
    for load in loads[:3]:
        load.start()
    digits = {
        name: lax.rem(lax.div(lax.axis_index(axis), unit), size)
        for name, (axis, unit, size) in PLACE.items()
    }
    rows_team, plane, line = (Team(names, digits) for names in TEAMS.values())
    signal_all((plane, line))
    phase = [0]
    copies = []

    def exchange(src, dst, team=rows_team, shared=False):
        at = phase[0]
        phase[0] += 1
        copies.append(Exchange(team, src, dst, send_sem.at[at], recv_sem.at[at], shared))
        return copies[-1]
    loads[0].wait()
    row0, col0 = pos[0, 0], pos[0, 1]

    pick = iota((n, length), 1) == iota((n, length), 0) + row0
    put[...] = pick.astype(F32).astype(BF16)
    group = iota((rows, LANES), 1) // width
    for load in loads[1:3]:
        load.wait()
    for load in loads[3:]:
        load.start()
    gap = jnp.zeros((LANES // 2 - cols, length), F32)
    block = jnp.concatenate([trans[0], gap, trans[1], gap], axis=0).astype(BF16)
    seen = dot_t(put[...], block)
    for d in range(grp):
        value = seen[rows * d : rows * (d + 1)]
        for h, at in enumerate(slots):
            t, g = per_part * h + d // groups, d % groups
            moved = pltpu.roll(meas[0, :, LANES * t : LANES * (t + 1)], (width * (at - g)) % LANES, 1)
            value = jnp.where(group == at, moved, value)
        x_send[d] = value.astype(BF16)
    x_recv[me] = x_send[me]

    wait_all((plane, line))
    x_copy = exchange(x_send, x_recv)
    x_copy.start()

    for d in range(grp):
        lane = iota((n, LANES), 1) % (LANES // 2)
        hit = (lane + cols * d == iota((n, LANES), 0) + col0) & (lane < cols)
        select[:, LANES * d : LANES * (d + 1)] = hit.astype(F32).astype(BF16)
    loads[3].wait()
    loads[4].wait()
    x_copy.wait_recv()
    first = iota((rows, LANES), 1) < LANES // 2
    stacked = []
    for d in range(grp):
        x = x_recv[d].astype(F32)
        zero = jnp.zeros_like(x)
        stacked.append(
            jnp.concatenate([jnp.where(first, x, zero), jnp.where(first, zero, x), zero, zero], axis=0).astype(BF16)
        )
    window = jnp.transpose(dot_t(select[...], jnp.concatenate(stacked, axis=1)))
    win_r, win_i = window[:rows], window[rows : 2 * rows]
    for m in range(modes):
        p_r, p_i = probe[0, m].astype(F32), probe[1, m].astype(F32)
        wave[0, rows * m : rows * (m + 1)] = (p_r * win_r - p_i * win_i).astype(BF16)
        wave[1, rows * m : rows * (m + 1)] = (p_r * win_i + p_i * win_r).astype(BF16)

    f_copies, b_copies = [], []
    for q in range(parts):
        span = slice(part * q, part * (q + 1))
        k_r, k_i = kmat[0, :, span], kmat[1, :, span]
        out = (
            dot(wave[0], k_r) - dot(wave[1], k_i),
            dot(wave[0], k_i) + dot(wave[1], k_r),
        )
        for c in range(2):
            for t in range(per_part):
                packed = swap(
                    [out[c][rows * m : rows * (m + 1), LANES * t : LANES * (t + 1)] for m in range(modes)]
                )
                for g in range(8):
                    f_send[q, 8 * t + g, :, LANES * c : LANES * (c + 1)] = packed[g].astype(BF16)
        f_recv[q, me] = f_send[q, me]
        f_copies.append(exchange(f_send.at[q], f_recv.at[q]))
        f_copies[q].start()

    seen = x_recv[...].astype(F32).reshape(n, LANES)
    group = iota((n, LANES), 1) // width
    for h, at in enumerate(slots):
        target[h] = spread_sum(jnp.where(group == at, seen, jnp.zeros_like(seen)), width)

    for load in loads[5:]:
        load.wait()
    spots = [
        (c, slice(8 * j, 8 * j + 8), slice(LANES * t, LANES * (t + 1)))
        for c in range(2)
        for j in range(cols // 8)
        for t in range(length // LANES)
    ]
    early, late = [], []
    for i in range(depth):
        early.append(("ss", i, i))
        late += [("sg", i, i), ("yg", i, i), ("sy", i, last), ("yy", i, last)]
        for j in range(i, last):
            early += [("sy", i, j), ("yy", i, j)]
    number = {name: at for at, name in enumerate(early + late)}

    def accumulate(names, vectors):
        sums = [None] * len(names)
        for at in spots:
            value = vectors(at)
            for e, (kind, a, b) in enumerate(names):
                left = value[kind[0]][a]
                right = value["g"] if kind[1] == "g" else value[kind[1]][b]
                sums[e] = left * right if sums[e] is None else sums[e] + left * right
        for name, total in zip(names, sums):
            gram[number[name] : number[name] + 1, :] = jnp.sum(total, axis=0, keepdims=True)

    def known(at):
        return {
            "s": [steps[(i, *at)] for i in range(depth)],
            "y": [changes[(i, *at)] for i in range(last)],
        }

    accumulate(early, known)

    for q in range(parts):
        f_copies[q].wait_recv()
        x = f_recv[q].reshape(n, 2 * LANES)
        by_r, by_i = dot(kmat[0], x), dot(kmat[1], x)
        d_r = (by_r[:, :LANES] - by_i[:, LANES:]).astype(BF16).astype(F32)
        d_i = (by_r[:, LANES:] + by_i[:, :LANES]).astype(BF16).astype(F32)
        misfit = spread_sum(d_r * d_r + d_i * d_i, width) - target[q]
        e = jnp.concatenate([(misfit * d_r).astype(BF16), (misfit * d_i).astype(BF16)], axis=1)
        by_r, by_i = dot(kmat[0], e), dot(kmat[1], e)
        b_send[q, :, :, :LANES] = (by_r[:, :LANES] + by_i[:, LANES:]).astype(BF16).reshape(grp, rows, LANES)
        b_send[q, :, :, LANES:] = (by_r[:, LANES:] - by_i[:, :LANES]).astype(BF16).reshape(grp, rows, LANES)
        b_recv[q, me] = b_send[q, me]
        b_copies.append(exchange(b_send.at[q], b_recv.at[q]))
        b_copies[q].start()

    place = iota((length, n), 0) == iota((length, n), 1) + col0
    shift[...] = place.astype(F32).astype(BF16)
    grad_r = jnp.zeros((rows, n), F32)
    grad_i = jnp.zeros((rows, n), F32)
    for q in range(parts):
        b_copies[q].wait_recv()
        back = []
        for c in range(2):
            by_tile = []
            for t in range(per_part):
                packed = swap(
                    [b_recv[q, 8 * t + g, :, LANES * c : LANES * (c + 1)].astype(F32) for g in range(8)]
                )
                by_tile.append(jnp.concatenate(packed, axis=0))
            back.append(jnp.concatenate(by_tile, axis=1).astype(BF16))
        span = slice(part * q, part * (q + 1))
        k_r, k_i = kmat[0, span, :], kmat[1, span, :]
        p_r = dot(back[0], k_r) + dot(back[1], k_i)
        p_i = dot(back[1], k_r) - dot(back[0], k_i)
        for m in range(modes):
            w_r, w_i = probe[0, m].astype(F32), probe[1, m].astype(F32)
            o_r, o_i = p_r[rows * m : rows * (m + 1)], p_i[rows * m : rows * (m + 1)]
            grad_r = grad_r + (w_r * o_r + w_i * o_i)
            grad_i = grad_i + (w_r * o_i - w_i * o_r)

    grad_r = (4.0 * grad_r).astype(BF16)
    grad_i = (4.0 * grad_i).astype(BF16)
    tall = dot_t(shift[...], jnp.concatenate([grad_r] * 4 + [grad_i] * 4, axis=0))
    tall = tall.reshape(grp, cols // 8, 8, 2 * LANES)
    pieces = [
        tall[:, j, :, LANES * c : LANES * (c + 1)] for c in range(2) for j in range(cols // 8)
    ]
    group = iota((grp, 8, LANES), 2) // 32
    zero = jnp.zeros((grp, 8, LANES), F32)
    wide = []
    for w in range(4):
        value = zero
        for p in range(4):
            if 4 * w + p < len(pieces):
                value = jnp.where(group == p, pieces[4 * w + p], value)
        wide.append(value)
    g_send[...] = jnp.concatenate(wide, axis=1).astype(BF16)
    g_recv[me] = g_send[me]
    g_copy = exchange(g_send, g_recv)
    g_copy.start()
    g_copy.wait_recv()
    for t in range(tiles):
        whole = [g_recv[4 * t + g].astype(F32) for g in range(4)]
        for w in range((len(pieces) + 3) // 4):
            packed = swap([x[8 * w : 8 * w + 8] for x in whole])
            for p in range(4):
                if 4 * w + p < len(pieces):
                    at = 8 * (4 * w + p)
                    tile[at : at + 8, LANES * t : LANES * (t + 1)] = packed[p]
    out = dot(tile[...].astype(BF16), put[...])
    data_ref[0] = out[:cols]
    data_ref[1] = out[cols:]

    def fresh(at):
        grad = data_ref[at] + TIKHONOV * trans[at]
        new = grad - old[at]
        gradient[at] = grad
        change[at] = new
        value = known(at)
        value["y"].append(new)
        value["g"] = grad
        return value

    accumulate(late, fresh)
    totals = jnp.sum(gram[...], axis=1, keepdims=True)
    count = gram.shape[0]
    totals = jnp.where(
        iota((count, LANES), 0) == iota((count, LANES), 1), totals, jnp.zeros((count, LANES), F32)
    )
    value = jnp.sum(totals, axis=0, keepdims=True)
    one_send[0] = value
    one_recv[plane.me] = value
    one = exchange(one_send.at[0], one_recv, plane, shared=True)
    one.start()
    one.wait_recv()
    value = jnp.sum(one_recv[...], axis=0)
    one_send[1] = value
    two_recv[line.me] = value
    two = exchange(one_send.at[1], two_recv, line, shared=True)
    two.start()
    two.wait_recv()
    value = jnp.sum(two_recv[...], axis=0)

    def inner(kind, a, b):
        at = number[(kind, a, b)]
        return jnp.broadcast_to(value[:, at : at + 1], (1, LANES))

    curve = [
        jnp.maximum(inner("sy", i, i), CURVE_FLOOR * inner("ss", i, i)) for i in range(depth)
    ]
    alphas = [None] * depth
    for i in reversed(range(depth)):
        along = inner("sg", i, i)
        for j in range(i + 1, depth):
            along = along - alphas[j] * inner("sy", i, j)
        alphas[i] = along / curve[i]
    scale = curve[last] / (inner("yy", last, last) + EPSILON)
    weights = []
    for i in range(depth):
        along = inner("yg", i, i)
        for j in range(depth):
            along = along - alphas[j] * inner("yy", min(i, j), max(i, j))
        along = scale * along
        for j in range(i):
            along = along + weights[j] * inner("sy", j, i)
        weights.append(alphas[i] - along / curve[i])
    wide = lambda x: jnp.broadcast_to(x, (8, LANES))
    alphas = [wide(scale * alpha) for alpha in alphas]
    weights = [wide(weight) for weight in weights]
    scale = wide(scale)
    for c in range(2):
        for at in spots:
            if at[0] != c:
                continue
            direction = scale * gradient[at]
            for i in range(depth):
                y = change[at] if i == last else changes[(i, *at)]
                direction = direction - alphas[i] * y + weights[i] * steps[(i, *at)]
            direction_ref[at] = direction
    for copy in copies:
        copy.wait_send()


def shards(grp, region, transmission, probe, measured, positions, past_steps, past_changes, old_gradient):
    two, cols, length = transmission.shape
    _, modes, rows, n = probe.shape
    parts = 2
    phases = 4 + 2 * parts
    hbm = pl.BlockSpec(memory_space=pltpu.HBM)
    shape = jax.ShapeDtypeStruct((two, cols, length), F32)
    block = (parts, grp, rows, 2 * LANES)
    data, direction = pl.pallas_call(
        functools.partial(step_kernel, grp, region),
        out_shape=(shape, shape),
        in_specs=[hbm] * 8,
        out_specs=(pl.BlockSpec(memory_space=pltpu.VMEM),) * 2,
        scratch_shapes=[
            pltpu.SMEM(positions.shape, jnp.int32),
            pltpu.VMEM((two, cols, length), F32),
            pltpu.VMEM(measured.shape, F32),
            pltpu.VMEM(probe.shape, BF16),
            pltpu.VMEM((2, n, n), BF16),
            pltpu.VMEM(past_steps.shape, F32),
            pltpu.VMEM(past_changes.shape, F32),
            pltpu.VMEM((two, cols, length), F32),
            pltpu.VMEM((grp, rows, LANES), BF16),
            pltpu.VMEM((grp, rows, LANES), BF16),
            pltpu.VMEM(block, BF16),
            pltpu.VMEM(block, BF16),
            pltpu.VMEM(block, BF16),
            pltpu.VMEM(block, BF16),
            pltpu.VMEM((grp, 32, LANES), BF16),
            pltpu.VMEM((grp, 32, LANES), BF16),
            pltpu.VMEM((2, 1, LANES), F32),
            pltpu.VMEM((2 * grp, 1, LANES), F32),
            pltpu.VMEM((region // 2, 1, LANES), F32),
            pltpu.VMEM((n, grp * LANES), BF16),
            pltpu.VMEM((n, length), BF16),
            pltpu.VMEM((2, modes * rows, n), BF16),
            pltpu.VMEM((parts, n, LANES), F32),
            pltpu.VMEM((length, n), BF16),
            pltpu.VMEM((two * cols, n), F32),
            pltpu.VMEM((32, LANES), F32),
            pltpu.VMEM((two, cols, length), F32),
            pltpu.VMEM((two, cols, length), F32),
            pltpu.SemaphoreType.DMA((8,)),
            pltpu.SemaphoreType.DMA((phases,)),
            pltpu.SemaphoreType.DMA((phases,)),
        ],
        compiler_params=pltpu.CompilerParams(
            collective_id=0, has_side_effects=True, vmem_limit_bytes=48 << 20
        ),
        name="step",
    )(
        *(
            pltpu.with_memory_space_constraint(operand, pltpu.HBM)
            for operand in (
                positions,
                transmission,
                measured,
                probe,
                jnp.asarray(propagator(n)),
                past_steps,
                past_changes,
                old_gradient,
            )
        )
    )
    return transmission - direction, data + TIKHONOV * transmission


def solution(mesh):
    return jax.shard_map(
        functools.partial(shards, mesh.shape["grp"], mesh.shape["region"]),
        mesh=mesh,
        in_specs=(
            P(None, "grp", "region"),
            P(None, None, "grp", None),
            P("region", "grp", None),
            P("region", None),
            P(None, None, "grp", "region"),
            P(None, None, "grp", "region"),
            P(None, "grp", "region"),
        ),
        out_specs=(P(None, "grp", "region"), P(None, "grp", "region")),
        check_vma=False,
    )
```

```python
import functools
import itertools
import math

import jax
import jax.numpy as jnp
import ml_dtypes
import numpy as np
from jax import lax
from jax.experimental import pallas as pl
from jax.experimental.pallas import tpu as pltpu
from jax.sharding import PartitionSpec as P

CURVE_FLOOR = 0.25
TIKHONOV = 0.5
EPSILON = 1e-06
F32 = jnp.float32
BF16 = jnp.bfloat16
LANES = 128


def propagator(count):
    index = np.arange(count)
    phase = np.outer(index, index) % count * (2.0 * np.pi / count)
    factor = 1.0 / np.sqrt(count)
    real = (np.cos(phase) * factor).astype(np.float32).astype(ml_dtypes.bfloat16)
    imag = (-np.sin(phase) * factor).astype(np.float32).astype(ml_dtypes.bfloat16)
    table = real.astype(np.float64) + 1j * imag.astype(np.float64)
    wavenumber = (index + count // 2) % count - count // 2
    chirp = np.exp(-2j * np.pi * (wavenumber * wavenumber % (4 * count)) / (4 * count))
    folded = (table * chirp[None, :]) @ table.conj()
    return np.stack([folded.real, folded.imag]).astype(np.float32).astype(ml_dtypes.bfloat16)


def dot(left, right):
    return jnp.dot(left, right, preferred_element_type=F32)


def dot_t(left, right):
    return lax.dot_general(left, right, (((1,), (1,)), ((), ())), preferred_element_type=F32)


def iota(shape, dim):
    return lax.broadcasted_iota(jnp.int32, shape, dim)


def swap(parts):
    count = len(parts)
    width = LANES // count
    lane = iota(parts[0].shape, 1)
    step = count // 2
    while step:
        low = lane % (2 * step * width) < step * width
        out = list(parts)
        for i in range(count):
            if i & step == 0:
                a, b = parts[i], parts[i + step]
                out[i] = jnp.where(low, a, pltpu.roll(b, step * width, 1))
                out[i + step] = jnp.where(low, pltpu.roll(a, LANES - step * width, 1), b)
        parts = out
        step //= 2
    return parts


def spread_sum(x, width):
    step = LANES // 2
    while step >= width:
        x = x + pltpu.roll(x, step, 1)
        step //= 2
    return x


PLACE = {
    "z": ("grp", 2, 8),
    "x_hi": ("grp", 1, 2),
    "y": ("region", 4, 8),
    "x_lo": ("region", 2, 2),
    "core": ("region", 1, 2),
}
TEAMS = {"rows": ("z", "x_hi"), "plane": ("z", "x_hi", "x_lo"), "line": ("y", "core")}


def hops(step):
    z, y = (min(step.get(name, 0), 8 - step.get(name, 0)) for name in ("z", "y"))
    x = 2 * step.get("x_hi", 0) + step.get("x_lo", 0)
    return z + y + min(x, 4 - x) + 0.25 * step.get("core", 0)


class Team:
    def __init__(self, names, digits):
        self.size = math.prod(PLACE[name][2] for name in names)
        self.me = 0
        for name in names:
            self.me = self.me * PLACE[name][2] + digits[name]
        steps = itertools.product(*(range(PLACE[name][2]) for name in names))
        steps = [dict(zip(names, step)) for step in steps if any(step)]
        self.hops, self.others = [], []
        for step in sorted(steps, key=lambda step: -hops(step)):
            place, number = {}, 0
            for name in names:
                axis, unit, size = PLACE[name]
                digit = lax.rem(digits[name] + step[name], size) if step[name] else digits[name]
                number = number * size + digit
            for axis in sorted({PLACE[name][0] for name in names}):
                place[axis] = sum(
                    (lax.rem(digits[name] + step[name], size) if step.get(name) else digits[name]) * unit
                    for name, (on, unit, size) in PLACE.items()
                    if on == axis
                )
            self.hops.append(hops(step))
            self.others.append((number, place))


class Exchange:
    def __init__(self, team, src, dst, send, recv, shared=False):
        self.team, self.src, self.dst = team, src, dst
        self.send, self.recv, self.shared = send, recv, shared

    def copy(self, src, dst, place):
        return pltpu.make_async_remote_copy(
            src_ref=src,
            dst_ref=dst,
            send_sem=self.send,
            recv_sem=self.recv,
            device_id=place,
            device_id_type=pl.DeviceIdType.MESH,
        )

    def start(self):
        for number, place in self.team.others:
            src = self.src if self.shared else self.src.at[number]
            self.copy(src, self.dst.at[self.team.me], place).start()

    def bulk(self):
        every = self.dst.at[pl.ds(0, self.team.size - 1)]
        return self.copy(every, every, self.team.others[0][1])

    def wait_recv(self):
        self.bulk().wait_recv()

    def wait_send(self):
        self.bulk().wait_send()


def signal_all(teams):
    sem = pltpu.get_barrier_semaphore()
    order = [(far, place) for team in teams for far, (_, place) in zip(team.hops, team.others)]
    for _, place in sorted(order, key=lambda item: -item[0]):
        pl.semaphore_signal(sem, inc=1, device_id=place, device_id_type=pl.DeviceIdType.MESH)


def wait_all(teams):
    pl.semaphore_wait(pltpu.get_barrier_semaphore(), sum(team.size - 1 for team in teams))


def step_kernel(
    grp,
    region,
    pos_hbm,
    trans_hbm,
    meas_hbm,
    probe_hbm,
    k_hbm,
    steps_hbm,
    changes_hbm,
    old_hbm,
    data_ref,
    direction_ref,
    pos,
    trans,
    meas,
    probe,
    kmat,
    steps,
    changes,
    old,
    x_send,
    x_recv,
    f_send,
    f_recv,
    b_send,
    b_recv,
    g_send,
    g_recv,
    one_send,
    one_recv,
    two_recv,
    select,
    put,
    wave,
    target,
    shift,
    tile,
    gram,
    gradient,
    change,
    load_sem,
    send_sem,
    recv_sem,
):
    me = lax.axis_index("grp")
    cols, length = trans.shape[1], trans.shape[2]
    modes, rows, n = probe.shape[1], probe.shape[2], probe.shape[3]
    tiles = n // LANES
    parts = 2
    width = n // (grp * parts)
    per_part = tiles // parts
    part = n // parts
    depth = steps.shape[0]
    last = depth - 1
    groups = LANES // width
    slots = (groups // 2 - 1, groups - 1)
    loads = [
        pltpu.make_async_copy(src, dst, load_sem.at[i])
        for i, (src, dst) in enumerate(
            (
                (pos_hbm, pos),
                (trans_hbm, trans),
                (meas_hbm, meas),
                (probe_hbm, probe),
                (k_hbm, kmat),
                (steps_hbm, steps),
                (changes_hbm, changes),
                (old_hbm, old),
            )
        )
    ]
    for load in loads[:3]:
        load.start()
    digits = {
        name: lax.rem(lax.div(lax.axis_index(axis), unit), size)
        for name, (axis, unit, size) in PLACE.items()
    }
    rows_team, plane, line = (Team(names, digits) for names in TEAMS.values())
    signal_all((plane, line))
    phase = [0]
    copies = []

    def exchange(src, dst, team=rows_team, shared=False):
        at = phase[0]
        phase[0] += 1
        copies.append(Exchange(team, src, dst, send_sem.at[at], recv_sem.at[at], shared))
        return copies[-1]
    loads[0].wait()
    row0, col0 = pos[0, 0], pos[0, 1]

    pick = iota((n, length), 1) == iota((n, length), 0) + row0
    put[...] = pick.astype(F32).astype(BF16)
    group = iota((rows, LANES), 1) // width
    for load in loads[1:3]:
        load.wait()
    for load in loads[3:]:
        load.start()
    gap = jnp.zeros((LANES // 2 - cols, length), F32)
    block = jnp.concatenate([trans[0], gap, trans[1], gap], axis=0).astype(BF16)
    seen = dot_t(put[...], block)
    for d in range(grp):
        value = seen[rows * d : rows * (d + 1)]
        for h, at in enumerate(slots):
            t, g = per_part * h + d // groups, d % groups
            moved = pltpu.roll(meas[0, :, LANES * t : LANES * (t + 1)], (width * (at - g)) % LANES, 1)
            value = jnp.where(group == at, moved, value)
        x_send[d] = value.astype(BF16)
    x_recv[me] = x_send[me]

    wait_all((plane, line))
    x_copy = exchange(x_send, x_recv)
    x_copy.start()

    for d in range(grp):
        lane = iota((n, LANES), 1) % (LANES // 2)
        hit = (lane + cols * d == iota((n, LANES), 0) + col0) & (lane < cols)
        select[:, LANES * d : LANES * (d + 1)] = hit.astype(F32).astype(BF16)
    loads[3].wait()
    loads[4].wait()
    x_copy.wait_recv()
    first = iota((rows, LANES), 1) < LANES // 2
    stacked = []
    for d in range(grp):
        x = x_recv[d].astype(F32)
        zero = jnp.zeros_like(x)
        stacked.append(
            jnp.concatenate([jnp.where(first, x, zero), jnp.where(first, zero, x)], axis=0).astype(BF16)
        )
    window = jnp.transpose(dot_t(select[...], jnp.concatenate(stacked, axis=1)))
    win_r, win_i = window[:rows], window[rows : 2 * rows]
    for m in range(modes):
        p_r, p_i = probe[0, m].astype(F32), probe[1, m].astype(F32)
        wave[0, rows * m : rows * (m + 1)] = (p_r * win_r - p_i * win_i).astype(BF16)
        wave[1, rows * m : rows * (m + 1)] = (p_r * win_i + p_i * win_r).astype(BF16)

    f_copies, b_copies = [], []
    for q in range(parts):
        span = slice(part * q, part * (q + 1))
        k_r, k_i = kmat[0, :, span], kmat[1, :, span]
        out = (
            dot(wave[0], k_r) - dot(wave[1], k_i),
            dot(wave[0], k_i) + dot(wave[1], k_r),
        )
        for c in range(2):
            for t in range(per_part):
                packed = swap(
                    [out[c][rows * m : rows * (m + 1), LANES * t : LANES * (t + 1)] for m in range(modes)]
                )
                for g in range(8):
                    f_send[q, 8 * t + g, :, LANES * c : LANES * (c + 1)] = packed[g].astype(BF16)
        f_recv[q, me] = f_send[q, me]
        f_copies.append(exchange(f_send.at[q], f_recv.at[q]))
        f_copies[q].start()

    seen = x_recv[...].astype(F32).reshape(n, LANES)
    group = iota((n, LANES), 1) // width
    for h, at in enumerate(slots):
        target[h] = spread_sum(jnp.where(group == at, seen, jnp.zeros_like(seen)), width)

    for load in loads[5:]:
        load.wait()
    spots = [
        (c, slice(8 * j, 8 * j + 8), slice(LANES * t, LANES * (t + 1)))
        for c in range(2)
        for j in range(cols // 8)
        for t in range(length // LANES)
    ]
    early, late = [], []
    for i in range(depth):
        early.append(("ss", i, i))
        late += [("sg", i, i), ("yg", i, i), ("sy", i, last), ("yy", i, last)]
        for j in range(i, last):
            early += [("sy", i, j), ("yy", i, j)]
    number = {name: at for at, name in enumerate(early + late)}

    def accumulate(names, vectors):
        sums = [None] * len(names)
        for at in spots:
            value = vectors(at)
            for e, (kind, a, b) in enumerate(names):
                left = value[kind[0]][a]
                right = value["g"] if kind[1] == "g" else value[kind[1]][b]
                sums[e] = left * right if sums[e] is None else sums[e] + left * right
        for name, total in zip(names, sums):
            gram[number[name] : number[name] + 1, :] = jnp.sum(total, axis=0, keepdims=True)

    def known(at):
        return {
            "s": [steps[(i, *at)] for i in range(depth)],
            "y": [changes[(i, *at)] for i in range(last)],
        }

    accumulate(early, known)

    for q in range(parts):
        f_copies[q].wait_recv()
        x = f_recv[q].reshape(n, 2 * LANES)
        by_r, by_i = dot(kmat[0], x), dot(kmat[1], x)
        d_r = (by_r[:, :LANES] - by_i[:, LANES:]).astype(BF16).astype(F32)
        d_i = (by_r[:, LANES:] + by_i[:, :LANES]).astype(BF16).astype(F32)
        misfit = spread_sum(d_r * d_r + d_i * d_i, width) - target[q]
        e = jnp.concatenate([(misfit * d_r).astype(BF16), (misfit * d_i).astype(BF16)], axis=1)
        by_r, by_i = dot(kmat[0], e), dot(kmat[1], e)
        b_send[q, :, :, :LANES] = (by_r[:, :LANES] + by_i[:, LANES:]).astype(BF16).reshape(grp, rows, LANES)
        b_send[q, :, :, LANES:] = (by_r[:, LANES:] - by_i[:, :LANES]).astype(BF16).reshape(grp, rows, LANES)
        b_recv[q, me] = b_send[q, me]
        b_copies.append(exchange(b_send.at[q], b_recv.at[q]))
        b_copies[q].start()

    place = iota((length, n), 0) == iota((length, n), 1) + col0
    shift[...] = place.astype(F32).astype(BF16)
    grad_r = jnp.zeros((rows, n), F32)
    grad_i = jnp.zeros((rows, n), F32)
    for q in range(parts):
        b_copies[q].wait_recv()
        back = []
        for c in range(2):
            by_tile = []
            for t in range(per_part):
                packed = swap(
                    [b_recv[q, 8 * t + g, :, LANES * c : LANES * (c + 1)].astype(F32) for g in range(8)]
                )
                by_tile.append(jnp.concatenate(packed, axis=0))
            back.append(jnp.concatenate(by_tile, axis=1).astype(BF16))
        span = slice(part * q, part * (q + 1))
        k_r, k_i = kmat[0, span, :], kmat[1, span, :]
        p_r = dot(back[0], k_r) + dot(back[1], k_i)
        p_i = dot(back[1], k_r) - dot(back[0], k_i)
        for m in range(modes):
            w_r, w_i = probe[0, m].astype(F32), probe[1, m].astype(F32)
            o_r, o_i = p_r[rows * m : rows * (m + 1)], p_i[rows * m : rows * (m + 1)]
            grad_r = grad_r + (w_r * o_r + w_i * o_i)
            grad_i = grad_i + (w_r * o_i - w_i * o_r)

    grad_r = (4.0 * grad_r).astype(BF16)
    grad_i = (4.0 * grad_i).astype(BF16)
    tall = dot_t(shift[...], jnp.concatenate([grad_r] * 4 + [grad_i] * 4, axis=0))
    tall = tall.reshape(grp, cols // 8, 8, 2 * LANES)
    pieces = [
        tall[:, j, :, LANES * c : LANES * (c + 1)] for c in range(2) for j in range(cols // 8)
    ]
    group = iota((grp, 8, LANES), 2) // 32
    zero = jnp.zeros((grp, 8, LANES), F32)
    wide = []
    for w in range((len(pieces) + 3) // 4):
        value = zero
        for p in range(4):
            if 4 * w + p < len(pieces):
                value = jnp.where(group == p, pieces[4 * w + p], value)
        wide.append(value)
    g_send[...] = jnp.concatenate(wide, axis=1).astype(BF16)
    g_recv[me] = g_send[me]
    g_copy = exchange(g_send, g_recv)
    g_copy.start()
    g_copy.wait_recv()
    for t in range(tiles):
        whole = [g_recv[4 * t + g].astype(F32) for g in range(4)]
        for w in range((len(pieces) + 3) // 4):
            packed = swap([x[8 * w : 8 * w + 8] for x in whole])
            for p in range(4):
                if 4 * w + p < len(pieces):
                    at = 8 * (4 * w + p)
                    tile[at : at + 8, LANES * t : LANES * (t + 1)] = packed[p]
    out = dot(tile[...].astype(BF16), put[...])
    data_ref[0] = out[:cols]
    data_ref[1] = out[cols:]

    def fresh(at):
        grad = data_ref[at] + TIKHONOV * trans[at]
        new = grad - old[at]
        gradient[at] = grad
        change[at] = new
        value = known(at)
        value["y"].append(new)
        value["g"] = grad
        return value

    accumulate(late, fresh)
    totals = jnp.sum(gram[...], axis=1, keepdims=True)
    count = gram.shape[0]
    totals = jnp.where(
        iota((count, LANES), 0) == iota((count, LANES), 1), totals, jnp.zeros((count, LANES), F32)
    )
    value = jnp.sum(totals, axis=0, keepdims=True)
    one_send[0] = value
    one_recv[plane.me] = value
    one = exchange(one_send.at[0], one_recv, plane, shared=True)
    one.start()
    one.wait_recv()
    value = jnp.sum(one_recv[...], axis=0)
    one_send[1] = value
    two_recv[line.me] = value
    two = exchange(one_send.at[1], two_recv, line, shared=True)
    two.start()
    two.wait_recv()
    value = jnp.sum(two_recv[...], axis=0)

    def inner(kind, a, b):
        at = number[(kind, a, b)]
        return jnp.broadcast_to(value[:, at : at + 1], (1, LANES))

    curve = [
        jnp.maximum(inner("sy", i, i), CURVE_FLOOR * inner("ss", i, i)) for i in range(depth)
    ]
    alphas = [None] * depth
    for i in reversed(range(depth)):
        along = inner("sg", i, i)
        for j in range(i + 1, depth):
            along = along - alphas[j] * inner("sy", i, j)
        alphas[i] = along / curve[i]
    scale = curve[last] / (inner("yy", last, last) + EPSILON)
    weights = []
    for i in range(depth):
        along = inner("yg", i, i)
        for j in range(depth):
            along = along - alphas[j] * inner("yy", min(i, j), max(i, j))
        along = scale * along
        for j in range(i):
            along = along + weights[j] * inner("sy", j, i)
        weights.append(alphas[i] - along / curve[i])
    wide = lambda x: jnp.broadcast_to(x, (8, LANES))
    alphas = [wide(scale * alpha) for alpha in alphas]
    weights = [wide(weight) for weight in weights]
    scale = wide(scale)
    for c in range(2):
        for at in spots:
            if at[0] != c:
                continue
            direction = scale * gradient[at]
            for i in range(depth):
                y = change[at] if i == last else changes[(i, *at)]
                direction = direction - alphas[i] * y + weights[i] * steps[(i, *at)]
            direction_ref[at] = direction
    for copy in copies:
        copy.wait_send()


def shards(grp, region, transmission, probe, measured, positions, past_steps, past_changes, old_gradient):
    two, cols, length = transmission.shape
    _, modes, rows, n = probe.shape
    parts = 2
    phases = 4 + 2 * parts
    hbm = pl.BlockSpec(memory_space=pltpu.HBM)
    shape = jax.ShapeDtypeStruct((two, cols, length), F32)
    block = (parts, grp, rows, 2 * LANES)
    data, direction = pl.pallas_call(
        functools.partial(step_kernel, grp, region),
        out_shape=(shape, shape),
        in_specs=[hbm] * 8,
        out_specs=(pl.BlockSpec(memory_space=pltpu.VMEM),) * 2,
        scratch_shapes=[
            pltpu.SMEM(positions.shape, jnp.int32),
            pltpu.VMEM((two, cols, length), F32),
            pltpu.VMEM(measured.shape, F32),
            pltpu.VMEM(probe.shape, BF16),
            pltpu.VMEM((2, n, n), BF16),
            pltpu.VMEM(past_steps.shape, F32),
            pltpu.VMEM(past_changes.shape, F32),
            pltpu.VMEM((two, cols, length), F32),
            pltpu.VMEM((grp, rows, LANES), BF16),
            pltpu.VMEM((grp, rows, LANES), BF16),
            pltpu.VMEM(block, BF16),
            pltpu.VMEM(block, BF16),
            pltpu.VMEM(block, BF16),
            pltpu.VMEM(block, BF16),
            pltpu.VMEM((grp, 24, LANES), BF16),
            pltpu.VMEM((grp, 24, LANES), BF16),
            pltpu.VMEM((2, 1, LANES), F32),
            pltpu.VMEM((2 * grp, 1, LANES), F32),
            pltpu.VMEM((region // 2, 1, LANES), F32),
            pltpu.VMEM((n, grp * LANES), BF16),
            pltpu.VMEM((n, length), BF16),
            pltpu.VMEM((2, modes * rows, n), BF16),
            pltpu.VMEM((parts, n, LANES), F32),
            pltpu.VMEM((length, n), BF16),
            pltpu.VMEM((two * cols, n), F32),
            pltpu.VMEM((32, LANES), F32),
            pltpu.VMEM((two, cols, length), F32),
            pltpu.VMEM((two, cols, length), F32),
            pltpu.SemaphoreType.DMA((8,)),
            pltpu.SemaphoreType.DMA((phases,)),
            pltpu.SemaphoreType.DMA((phases,)),
        ],
        compiler_params=pltpu.CompilerParams(
            collective_id=0, has_side_effects=True, vmem_limit_bytes=48 << 20
        ),
        name="step",
    )(
        *(
            pltpu.with_memory_space_constraint(operand, pltpu.HBM)
            for operand in (
                positions,
                transmission,
                measured,
                probe,
                jnp.asarray(propagator(n)),
                past_steps,
                past_changes,
                old_gradient,
            )
        )
    )
    return transmission - direction, data + TIKHONOV * transmission


def solution(mesh):
    return jax.shard_map(
        functools.partial(shards, mesh.shape["grp"], mesh.shape["region"]),
        mesh=mesh,
        in_specs=(
            P(None, "grp", "region"),
            P(None, None, "grp", None),
            P("region", "grp", None),
            P("region", None),
            P(None, None, "grp", "region"),
            P(None, None, "grp", "region"),
            P(None, "grp", "region"),
        ),
        out_specs=(P(None, "grp", "region"), P(None, "grp", "region")),
        check_vma=False,
    )
```
